32 devices in a mesh: cond: 4 (over y, x), slab: 8 (over z, core).
Axes of the slice: x: 2, y: 2, z: 4, core: 2. Of those that a mesh axis runs over, the one named last changes fastest.
Arguments:
- mask_pixels: int32 [2048, 2048], P('slab'), may hold values 0 or 1
- target_bits: int32 [2048, 2048], P('slab'), may hold values 0 or 1
- perturb: float32 [2048, 2048], P('slab'), may hold values from -1.5 to 1.5
- diffusivity: float32 [2048, 2048], P('slab'), may hold values from 0.03 to 0.24
- kernels: float32 [4, 8, 2, 128, 128], P('cond'), may hold values from -6 to 6
- cond_ids: int32 [4], P('cond'), may hold values from 0 to 15
- dose_table: float32 [16], replicated, may hold values from 0.7 to 1.3
Outputs:
- mask_grad: float32 [2048, 2048], P('slab')
The draws below stay inside these ranges and needn't reach their ends.
All inputs are finite; a program needn't handle non-finite values. No bound on the sum of `mask_pixels` or of `target_bits` on one device may be relied on, other than what follows from the above.
Results may differ from the reference program's by a relative error of at most 0.0003.
Values sent between devices are 32-bit elements; how exact they have to be, the bound alone decides.
A program may use at most 192 MiB of HBM per device.

```python
import math
import jax
import jax.numpy as jnp
from jax import lax

N = 2048
B = 128
KERN = 8
STEPS = 4
TABLE = 16
CONDS = 4


def set_ends(drawn, key, least, largest):
    extent = drawn.shape
    spot = [jax.random.randint(jax.random.fold_in(key, axis), (), 0, extent[axis]) for axis in range(len(extent))]
    drawn = drawn.at[tuple(spot)].set(least)
    longest = extent.index(max(extent))
    spot[longest] = (spot[longest] + 1) % extent[longest]
    return drawn.at[tuple(spot)].set(largest)


def level_of(rng, dims, cuts, low, top_value):
    def one(axis_at, parts):
        draws = jax.random.uniform(jax.random.fold_in(jax.random.fold_in(rng, 6), axis_at), (parts,), jnp.float32, low / len(cuts), top_value / len(cuts))
        return jnp.repeat(jnp.exp(draws), dims[axis_at] // parts).reshape((-1,) + (1,) * (len(dims) - axis_at - 1))

    factor_of = one(*cuts[0])
    for cut in cuts[1:]:
        factor_of = factor_of * one(*cut)
    return factor_of


def scatter_about(rng, shape, scale, most, cuts=(), kind=jnp.bfloat16):
    result = scale * jax.random.normal(rng, shape, jnp.float32)
    if cuts:
        result = result * level_of(rng, shape, cuts, -0.22, 0.18)
    return jnp.clip(result, -most, most).astype(kind)


def setup_inputs(seed: int = 0) -> dict:
    key_of = jax.random.split(jax.random.key(seed), 8)
    mask_pixels = set_ends((jax.random.randint(key_of[0], (N, N), 0, 2) < 1).astype(jnp.int32), jax.random.fold_in(key_of[0], 1), 0, 1)
    target_bits = set_ends((jax.random.randint(key_of[1], (N, N), 0, 2) < 1).astype(jnp.int32), jax.random.fold_in(key_of[1], 1), 0, 1)
    perturb = jnp.clip(jax.random.uniform(key_of[2], (N, N), jnp.float32, -1.5, 1.5) * level_of(key_of[2], (N, N), ((0, 8),), -0.4, 0.0), -1.5, 1.5)
    diffusivity = jnp.clip(jnp.exp(math.log(0.24) - 2.0794415 * jax.random.uniform(key_of[3], (N, N), jnp.float32) ** level_of(key_of[3], (N, N), ((0, 8),), -0.2, 0.2)), 0.03, 0.24)
    kernels = scatter_about(key_of[4], (CONDS, KERN, 2, B, B), 0.9, 6.0, ((0, 4),), jnp.float32)
    cond_ids = set_ends(jax.random.randint(key_of[5], (CONDS,), 0, TABLE), jax.random.fold_in(key_of[5], 1), 0, TABLE - 1).astype(jnp.int32)
    dose_table = jnp.clip(jax.random.uniform(key_of[6], (TABLE,), jnp.float32, 0.7, 1.3), 0.7, 1.3)
    return dict(mask_pixels=mask_pixels, target_bits=target_bits, perturb=perturb, diffusivity=diffusivity, kernels=kernels, cond_ids=cond_ids, dose_table=dose_table)


precise = lax.Precision.HIGHEST
steepness = 4.0
threshold = 1.0
theta_scale = 2.5


def angle_tables(cell_index, length, band_size):
    frequency = jnp.arange(band_size, dtype=jnp.int32) - band_size // 2
    turn_count = (cell_index[:, None] * frequency[None, :]) % length
    phase_angle = turn_count.astype(jnp.float32) * (2.0 * math.pi / length)
    return jnp.cos(phase_angle), jnp.sin(phase_angle)


def wide_table(cos_cols, sin_cols):
    upper_half = jnp.concatenate([cos_cols.T, sin_cols.T], axis=1)
    lower_half = jnp.concatenate([-sin_cols.T, cos_cols.T], axis=1)
    return jnp.concatenate([upper_half, lower_half], axis=0)


def diffuse_periodic(field, coefficient):
    upper_rows = jnp.roll(field, 1, 0)
    lower_rows = jnp.roll(field, -1, 0)
    left_side = jnp.roll(field, 1, 1)
    right_side = jnp.roll(field, -1, 1)
    return (field
            + 0.5 * (coefficient + jnp.roll(coefficient, 1, 0)) * (upper_rows - field)
            + 0.5 * (coefficient + jnp.roll(coefficient, -1, 0)) * (lower_rows - field)
            + 0.5 * (coefficient + jnp.roll(coefficient, 1, 1)) * (left_side - field)
            + 0.5 * (coefficient + jnp.roll(coefficient, -1, 1)) * (right_side - field))


def bake_periodic(field, coefficient):
    for sweep_index in range(STEPS):
        field = diffuse_periodic(field, coefficient)
    return field


def reference(mask_pixels, target_bits, perturb, diffusivity, kernels, cond_ids, dose_table):
    cos_table, sin_table = angle_tables(jnp.arange(N, dtype=jnp.int32), N, B)
    project_table = jnp.concatenate([cos_table, -sin_table], axis=1)
    spread_table = wide_table(cos_table, sin_table)
    theta_field = theta_scale * (2.0 * mask_pixels.astype(jnp.float32) - 1.0) + perturb
    transmission = jnp.tanh(0.5 * theta_field)
    projected = jnp.dot(transmission, project_table, precision=precise, preferred_element_type=jnp.float32)
    proj_real = projected[:, :B]
    proj_imag = projected[:, B:]
    band_real = (jnp.dot(cos_table.T, proj_real, precision=precise, preferred_element_type=jnp.float32)
                 + jnp.dot(sin_table.T, proj_imag, precision=precise, preferred_element_type=jnp.float32)) / N
    band_imag = (jnp.dot(cos_table.T, proj_imag, precision=precise, preferred_element_type=jnp.float32)
                 - jnp.dot(sin_table.T, proj_real, precision=precise, preferred_element_type=jnp.float32)) / N
    target_field = target_bits.astype(jnp.float32)
    levels = jnp.arange(TABLE, dtype=jnp.int32)

    def one_condition(pair):
        kern_local, cond_one = pair
        dose_level = jnp.sum(dose_table * (levels == cond_one).astype(jnp.float32))
        kern_real = kern_local[:, 0]
        kern_imag = kern_local[:, 1]
        field_real = kern_real * band_real - kern_imag * band_imag
        field_imag = kern_real * band_imag + kern_imag * band_real
        rows_real = (jnp.einsum('xu,kuv->kxv', cos_table, field_real, precision=precise)
                     - jnp.einsum('xu,kuv->kxv', sin_table, field_imag, precision=precise))
        rows_imag = (jnp.einsum('xu,kuv->kxv', cos_table, field_imag, precision=precise)
                     + jnp.einsum('xu,kuv->kxv', sin_table, field_real, precision=precise))
        stacked = jnp.concatenate([rows_real, rows_imag], axis=-1).reshape(KERN * N, 2 * B)
        fields = (jnp.dot(stacked, spread_table, precision=precise, preferred_element_type=jnp.float32) / B).reshape(KERN, N, 2 * N)
        squares = jnp.sum(fields * fields, axis=0)
        intensity = dose_level / KERN * (squares[:, :N] + squares[:, N:])
        acid_field = bake_periodic(intensity, diffusivity)
        resist = jax.nn.sigmoid(steepness * (acid_field - threshold))
        acid_grad = steepness * (resist - target_field) * resist * (1.0 - resist)
        intensity_grad = bake_periodic(acid_grad, diffusivity)
        doubled = jnp.concatenate([intensity_grad, intensity_grad], axis=1)
        field_grad = (2.0 * dose_level / KERN) * fields * doubled[None]
        adjoint = lax.dot_general(spread_table, field_grad.reshape(KERN * N, 2 * N), (((1,), (1,)), ((), ())),
                                  precision=precise, preferred_element_type=jnp.float32) / B
        columns = adjoint.reshape(2, B, KERN, N)
        grad_real = (jnp.einsum('xu,vkx->kuv', cos_table, columns[0], precision=precise)
                     + jnp.einsum('xu,vkx->kuv', sin_table, columns[1], precision=precise))
        grad_imag = (jnp.einsum('xu,vkx->kuv', cos_table, columns[1], precision=precise)
                     - jnp.einsum('xu,vkx->kuv', sin_table, columns[0], precision=precise))
        return jnp.stack([jnp.sum(kern_real * grad_real + kern_imag * grad_imag, axis=0),
                          jnp.sum(kern_real * grad_imag - kern_imag * grad_real, axis=0)])

    per_cond = lax.map(one_condition, (kernels, cond_ids))
    band_grad = jnp.sum(per_cond, axis=0)
    back_real = (jnp.dot(cos_table, band_grad[0], precision=precise, preferred_element_type=jnp.float32)
                 - jnp.dot(sin_table, band_grad[1], precision=precise, preferred_element_type=jnp.float32)) / N
    back_imag = (jnp.dot(sin_table, band_grad[0], precision=precise, preferred_element_type=jnp.float32)
                 + jnp.dot(cos_table, band_grad[1], precision=precise, preferred_element_type=jnp.float32)) / N
    trans_grad = lax.dot_general(jnp.concatenate([back_real, back_imag], axis=1), project_table,
                                 (((1,), (1,)), ((), ())), precision=precise, preferred_element_type=jnp.float32)
    return trans_grad * 0.5 * (1.0 - transmission * transmission)
```

```python
import functools
import math

import jax
import jax.numpy as jnp
import numpy as np
from jax import lax
from jax.experimental import pallas as pl
from jax.experimental.pallas import tpu as pltpu
from jax.sharding import PartitionSpec as P

STEPS = 4
HALO = 2 * STEPS

steepness = 4.0
threshold = 1.0
theta_scale = 2.5

f32 = jnp.float32
bf16 = jnp.bfloat16
VMEM = pl.BlockSpec(memory_space=pltpu.VMEM)
SMEM = pl.BlockSpec(memory_space=pltpu.SMEM)
NN = (((1,), (0,)), ((), ()))
NT = (((1,), (1,)), ((), ()))
TN = (((0,), (0,)), ((), ()))


def split_np(table):
    high = table.astype(bf16)
    low = (table - high.astype(np.float64)).astype(bf16)
    return jnp.asarray(high), jnp.asarray(low)


def coarse_tables(band):
    points = 2 * band
    turns = np.arange(points)[:, None] * (np.arange(band)[None, :] - band // 2) % points
    angle = turns * (2.0 * math.pi / points)
    cos, sin = np.cos(angle), np.sin(angle)
    return np.concatenate(
        [np.concatenate([cos, -sin], 1), np.concatenate([sin, cos], 1)], 0
    )


def interpolation_table(length, band):
    points = 2 * band
    fine = np.arange(-HALO, length + HALO)
    scale = length // points
    offset = (fine[:, None] - scale * np.arange(points)[None, :]) % length
    freq = np.arange(1, band)
    profile = 1.0 + 2.0 * np.cos(
        (np.arange(length)[:, None] * freq[None, :] % length) * (2.0 * math.pi / length)
    ).sum(1)
    return profile[offset] / points


def angle_parts(length, band, inner):
    freq = np.arange(band) - band // 2
    fine = (np.arange(inner)[:, None] * freq % length) * (2.0 * math.pi / length)
    jump = (np.arange(length // inner)[:, None] * inner * freq % length) * (
        2.0 * math.pi / length
    )
    small = np.stack([np.cos(fine), np.sin(fine)]).astype(np.float32)
    large = np.stack([np.cos(jump), np.sin(jump)]).astype(np.float32)
    return jnp.asarray(small), jnp.asarray(large)


def halves(value):
    high = value.astype(bf16)
    return high, (value - high.astype(f32)).astype(bf16)


def dot3(left, right, dims=NN):
    go = lambda a, b: lax.dot_general(a, b, dims, preferred_element_type=f32)
    return go(left[0], right[0]) + (go(left[0], right[1]) + go(left[1], right[0]))


def project_kernel(mask, perturb, small, large, trans, tab_h, tab_l, band_out, acc):
    rows, length = mask.shape
    band = small.shape[2]
    inner = small.shape[1]
    cos_b, sin_b = small[0], small[1]

    @pl.loop(0, length // inner)
    def _(step):
        cos_a = large[0, pl.ds(step, 1), :]
        sin_a = large[1, pl.ds(step, 1), :]
        at = pl.ds(pl.multiple_of(step * inner, inner), inner)
        for part, value in (
            (0, cos_a * cos_b - sin_a * sin_b),
            (1, -(sin_a * cos_b + cos_a * sin_b)),
        ):
            high, low = halves(value)
            tab_h[at, part * band : (part + 1) * band] = high
            tab_l[at, part * band : (part + 1) * band] = low

    acc[...] = jnp.zeros_like(acc)
    wide = 256

    @pl.loop(0, length // wide)
    def _(step):
        at = pl.ds(pl.multiple_of(step * wide, wide), wide)
        theta = theta_scale * (2.0 * mask[:, at].astype(f32) - 1.0) + perturb[:, at]
        value = jnp.tanh(0.5 * theta)
        trans[:, at] = value
        acc[...] += dot3(halves(value), (tab_h[at, :], tab_l[at, :]))

    mine = pl.ds(pl.multiple_of(lax.axis_index("slab") * rows, rows), rows)
    mixed = dot3((tab_h[mine, :], tab_l[mine, :]), halves(acc[...] / length), TN)
    band_out[0:band, :] = mixed[0:band, 0:band] - mixed[band:, band:]
    band_out[band:, :] = mixed[0:band, band:] + mixed[band:, 0:band]


def bake_sweep(field, vert, horiz, row_mask):
    total, length = field.shape
    chunks = total // 8

    def body(index, carry):
        at = pl.ds(pl.multiple_of(index * 8, 8), 8)
        after = pl.ds(pl.multiple_of(jnp.minimum(index + 1, chunks - 1) * 8, 8), 8)
        here = field[at, :]
        there = field[after, :]
        last = row_mask == 7
        below = jnp.where(last, pltpu.roll(there, 7, 0), pltpu.roll(here, 7, 0))
        flow = vert[at, :] * (below - here)
        rolled = pltpu.roll(flow, 1, 0)
        above = jnp.where(row_mask == 0, carry, rolled)
        side = horiz[at, :] * (pltpu.roll(here, length - 1, 1) - here)
        field[at, :] = here + (flow - above) + (side - pltpu.roll(side, 1, 1))
        return rolled

    lax.fori_loop(0, chunks, body, jnp.zeros((8, length), f32))


def image_kernel(
    band_in, kern, dose, diff, target, lh, ll, th, tl, wh, wl, out,
    ah, al, mid, fields, coarse, field, vert, horiz, zh, zl, grad, qh, ql,
):
    count, _, band, _ = kern.shape
    total, length = diff.shape
    rows = total - 2 * HALO
    points = 2 * band
    level = dose[0, 0]
    first = pl.multiple_of(lax.axis_index("slab") * rows, rows)
    row_mask = lax.broadcasted_iota(jnp.int32, (8, length), 0)
    chunks = total // 8

    @pl.loop(0, chunks)
    def _(index):
        at = pl.ds(pl.multiple_of(index * 8, 8), 8)
        after = pl.ds(pl.multiple_of(jnp.minimum(index + 1, chunks - 1) * 8, 8), 8)
        here = diff[at, :]
        below = jnp.where(
            row_mask == 7, pltpu.roll(diff[after, :], 7, 0), pltpu.roll(here, 7, 0)
        )
        vert[at, :] = 0.5 * (here + below)
        horiz[at, :] = 0.5 * (here + pltpu.roll(here, length - 1, 1))

    real, imag = band_in[0:band, :], band_in[band:, :]
    for k in range(count):
        cols = slice(k * band, (k + 1) * band)
        kr, ki = kern[k, 0], kern[k, 1]
        ah[0:band, cols], al[0:band, cols] = halves(kr * real - ki * imag)
        ah[band:, cols], al[band:, cols] = halves(kr * imag + ki * real)

    @pl.loop(0, count // 2)
    def _(pair):
        at = pl.ds(pl.multiple_of(pair * points, points), points)
        mid[:, at] = dot3((lh[...], ll[...]), (ah[:, at], al[:, at]))

    coarse[...] = jnp.zeros_like(coarse)

    @pl.loop(0, count)
    def _(k):
        at = pl.ds(pl.multiple_of(k * band, band), band)
        block = jnp.concatenate([mid[0:points, at], mid[points:, at]], axis=1)
        value = dot3(halves(block), (th[...], tl[...])) * (1.0 / band)
        fields[k] = value
        re, im = value[:, :points], value[:, points:]
        coarse[...] += re * re + im * im

    near = pl.ds(first, total)
    zh[...], zl[...] = halves(
        dot3((wh[near, :], wl[near, :]), halves(coarse[...] * (level / count)))
    )
    wide = 256

    @pl.loop(0, length // wide)
    def _(step):
        at = pl.ds(pl.multiple_of(step * wide, wide), wide)
        src = pl.ds(pl.multiple_of(step * wide + HALO, HALO), wide)
        field[:, at] = dot3((zh[...], zl[...]), (wh[src, :], wl[src, :]), NT)

    @pl.loop(0, STEPS)
    def _(sweep):
        bake_sweep(field, vert, horiz, row_mask)

    @pl.loop(0, chunks)
    def _(index):
        at = pl.ds(pl.multiple_of(index * 8, 8), 8)
        resist = jax.nn.sigmoid(steepness * (field[at, :] - threshold))
        field[at, :] = (
            steepness * (resist - target[at, :].astype(f32)) * resist * (1.0 - resist)
        )

    @pl.loop(0, STEPS)
    def _(sweep):
        bake_sweep(field, vert, horiz, row_mask)

    grad[...] = jnp.zeros_like(grad)

    @pl.loop(0, length // wide)
    def _(step):
        at = pl.ds(pl.multiple_of(step * wide, wide), wide)
        src = pl.ds(pl.multiple_of(step * wide + HALO, HALO), wide)
        grad[...] += dot3(
            halves(field[HALO : HALO + rows, at]), (wh[src, :], wl[src, :])
        )

    inside = pl.ds(pl.multiple_of(first + HALO, HALO), rows)
    spread = dot3((wh[inside, :], wl[inside, :]), halves(grad[...]), TN)
    coarse[...] = spread * (2.0 * level / count / band)

    @pl.loop(0, count)
    def _(k):
        at = pl.ds(pl.multiple_of(k * band, band), band)
        weight = coarse[...]
        block = fields[k] * jnp.concatenate([weight, weight], axis=1)
        back = dot3(halves(block), (lh[...], ll[...]))
        qh[0:points, at], ql[0:points, at] = halves(back[:, :band])
        qh[points:, at], ql[points:, at] = halves(back[:, band:])

    @pl.loop(0, count // 2)
    def _(pair):
        at = pl.ds(pl.multiple_of(pair * points, points), points)
        mid[0:points, at] = dot3((th[...], tl[...]), (qh[:, at], ql[:, at]))

    sum_re = jnp.zeros((band, band), f32)
    sum_im = jnp.zeros((band, band), f32)
    for k in range(count):
        cols = slice(k * band, (k + 1) * band)
        kr, ki = kern[k, 0], kern[k, 1]
        gr, gi = mid[0:band, cols], mid[band:points, cols]
        sum_re += kr * gr + ki * gi
        sum_im += kr * gi - ki * gr
    out[0:band, :] = sum_re
    out[band:, :] = sum_im


def final_kernel(grad, trans, tab_h, tab_l, out, bh, bl):
    rows, length = trans.shape
    band = grad.shape[1]
    top, low = grad[0:band, :], grad[band:, :]
    matrix = jnp.concatenate(
        [jnp.concatenate([top, low], 1), jnp.concatenate([low, -top], 1)], 0
    )
    mine = pl.ds(pl.multiple_of(lax.axis_index("slab") * rows, rows), rows)
    bh[...], bl[...] = halves(
        dot3((tab_h[mine, :], tab_l[mine, :]), halves(matrix)) * (0.5 / length)
    )
    wide = 256

    @pl.loop(0, length // wide)
    def _(step):
        at = pl.ds(pl.multiple_of(step * wide, wide), wide)
        value = dot3((bh[...], bl[...]), (tab_h[at, :], tab_l[at, :]), NT)
        t = trans[:, at]
        out[:, at] = value * (1.0 - t * t)


def with_halo(cells, width):
    count = lax.axis_size("slab")
    head = cells[:width]
    tail = cells[cells.shape[0] - width :]
    return jnp.concatenate(
        [
            lax.ppermute(tail, "slab", [(i, (i + 1) % count) for i in range(count)]),
            cells,
            lax.ppermute(head, "slab", [((i + 1) % count, i) for i in range(count)]),
        ],
        axis=0,
    )


def shape(dims, kind=f32):
    return jax.ShapeDtypeStruct(dims, kind)


def shards(mask_pixels, target_bits, perturb, diffusivity, kernels, cond_ids, dose_table):
    rows, length = mask_pixels.shape
    count, band = kernels.shape[1], kernels.shape[-1]
    points = 2 * band
    total = rows + 2 * HALO
    params = pltpu.CompilerParams(vmem_limit_bytes=60 * 1024 * 1024)
    small, large = angle_parts(length, band, 64)
    left = coarse_tables(band)
    lh, ll = split_np(left)
    th, tl = split_np(np.ascontiguousarray(left.T))
    wh, wl = split_np(interpolation_table(length, band))
    trans, tab_h, tab_l, local = pl.pallas_call(
        project_kernel,
        out_shape=(
            shape((rows, length)),
            shape((length, points), bf16),
            shape((length, points), bf16),
            shape((points, band)),
        ),
        in_specs=[VMEM] * 4,
        out_specs=(VMEM,) * 4,
        scratch_shapes=[pltpu.VMEM((rows, points), f32)],
        compiler_params=params,
        name="project",
    )(mask_pixels, perturb, small, large)
    mask_band = lax.psum(local, "slab")
    levels = jnp.arange(dose_table.shape[0], dtype=jnp.int32)
    dose = jnp.sum(dose_table * (levels == cond_ids[0]).astype(f32)).reshape(1, 1)
    diff = with_halo(diffusivity, HALO)
    target = with_halo(target_bits, HALO)
    part = pl.pallas_call(
        image_kernel,
        out_shape=shape((points, band)),
        in_specs=[VMEM] * 2 + [SMEM] + [VMEM] * 8,
        out_specs=VMEM,
        scratch_shapes=[
            pltpu.VMEM((points, count * band), bf16),
            pltpu.VMEM((points, count * band), bf16),
            pltpu.VMEM((2 * points, count * band), f32),
            pltpu.VMEM((count, points, 2 * points), f32),
            pltpu.VMEM((points, points), f32),
            pltpu.VMEM((total, length), f32),
            pltpu.VMEM((total, length), f32),
            pltpu.VMEM((total, length), f32),
            pltpu.VMEM((total, points), bf16),
            pltpu.VMEM((total, points), bf16),
            pltpu.VMEM((rows, points), f32),
            pltpu.VMEM((2 * points, count * band), bf16),
            pltpu.VMEM((2 * points, count * band), bf16),
        ],
        compiler_params=params,
        name="image",
    )(mask_band, kernels[0], dose, diff, target, lh, ll, th, tl, wh, wl)
    grad = lax.psum(part, ("cond", "slab"))
    return pl.pallas_call(
        final_kernel,
        out_shape=shape((rows, length)),
        in_specs=[VMEM] * 4,
        out_specs=VMEM,
        scratch_shapes=[
            pltpu.VMEM((rows, points), bf16),
            pltpu.VMEM((rows, points), bf16),
        ],
        compiler_params=params,
        name="final",
    )(grad, trans, tab_h, tab_l)


def solution(mesh):
    placed = (
        P("slab", None),
        P("slab", None),
        P("slab", None),
        P("slab", None),
        P("cond", None, None, None, None),
        P("cond"),
        P(),
    )
    return jax.shard_map(
        shards, mesh=mesh, in_specs=placed, out_specs=P("slab", None), check_vma=False
    )
```

```python
import functools
import math

import jax
import jax.numpy as jnp
import numpy as np
from jax import lax
from jax.experimental import pallas as pl
from jax.experimental.pallas import tpu as pltpu
from jax.sharding import PartitionSpec as P

STEPS = 4
HALO = 2 * STEPS

steepness = 4.0
threshold = 1.0
theta_scale = 2.5

f32 = jnp.float32
bf16 = jnp.bfloat16
VMEM = pl.BlockSpec(memory_space=pltpu.VMEM)
ANY = pl.BlockSpec(memory_space=pl.ANY)
MESH = pl.DeviceIdType.MESH
SMEM = pl.BlockSpec(memory_space=pltpu.SMEM)
NN = (((1,), (0,)), ((), ()))
NT = (((1,), (1,)), ((), ()))
TN = (((0,), (0,)), ((), ()))


def split_np(table):
    high = table.astype(bf16)
    low = (table - high.astype(np.float64)).astype(bf16)
    return jnp.asarray(high), jnp.asarray(low)


def coarse_tables(band):
    points = 2 * band
    turns = np.arange(points)[:, None] * (np.arange(band)[None, :] - band // 2) % points
    angle = turns * (2.0 * math.pi / points)
    cos, sin = np.cos(angle), np.sin(angle)
    return np.concatenate(
        [np.concatenate([cos, -sin], 1), np.concatenate([sin, cos], 1)], 0
    )


def interpolation_table(length, band):
    points = 2 * band
    fine = np.arange(-HALO, length + HALO)
    scale = length // points
    offset = (fine[:, None] - scale * np.arange(points)[None, :]) % length
    freq = np.arange(1, band)
    profile = 1.0 + 2.0 * np.cos(
        (np.arange(length)[:, None] * freq[None, :] % length) * (2.0 * math.pi / length)
    ).sum(1)
    return profile[offset] / points


def angle_parts(length, band, inner):
    freq = np.arange(band) - band // 2
    fine = (np.arange(inner)[:, None] * freq % length) * (2.0 * math.pi / length)
    jump = (np.arange(length // inner)[:, None] * inner * freq % length) * (
        2.0 * math.pi / length
    )
    small = np.stack([np.cos(fine), np.sin(fine)]).astype(np.float32)
    large = np.stack([np.cos(jump), np.sin(jump)]).astype(np.float32)
    return jnp.asarray(small), jnp.asarray(large)


def halves(value):
    high = value.astype(bf16)
    return high, (value - high.astype(f32)).astype(bf16)


def dot3(left, right, dims=NN):
    go = lambda a, b: lax.dot_general(a, b, dims, preferred_element_type=f32)
    return go(left[0], right[0]) + (go(left[0], right[1]) + go(left[1], right[0]))


def project_kernel(mask, perturb, small, large, trans, tab_h, tab_l, band_out, acc):
    rows, length = mask.shape
    band = small.shape[2]
    inner = small.shape[1]
    cos_b, sin_b = small[0], small[1]

    @pl.loop(0, length // inner)
    def _(step):
        cos_a = large[0, pl.ds(step, 1), :]
        sin_a = large[1, pl.ds(step, 1), :]
        at = pl.ds(pl.multiple_of(step * inner, inner), inner)
        for part, value in (
            (0, cos_a * cos_b - sin_a * sin_b),
            (1, -(sin_a * cos_b + cos_a * sin_b)),
        ):
            high, low = halves(value)
            tab_h[at, part * band : (part + 1) * band] = high
            tab_l[at, part * band : (part + 1) * band] = low

    acc[...] = jnp.zeros_like(acc)
    wide = 256

    @pl.loop(0, length // wide)
    def _(step):
        at = pl.ds(pl.multiple_of(step * wide, wide), wide)
        theta = theta_scale * (2.0 * mask[:, at].astype(f32) - 1.0) + perturb[:, at]
        value = jnp.tanh(0.5 * theta)
        trans[:, at] = value
        acc[...] += dot3(halves(value), (tab_h[at, :], tab_l[at, :]))

    mine = pl.ds(pl.multiple_of(lax.axis_index("slab") * rows, rows), rows)
    mixed = dot3((tab_h[mine, :], tab_l[mine, :]), halves(acc[...] / length), TN)
    band_out[0:band, :] = mixed[0:band, 0:band] - mixed[band:, band:]
    band_out[band:, :] = mixed[0:band, band:] + mixed[band:, 0:band]


def bake_sweep(source, dest, coeffs, row_mask):
    east, west, north, south, middle = coeffs
    total, length = middle.shape
    chunks = total // 8
    unroll = max(d for d in range(1, 18) if chunks % d == 0)

    @pl.loop(0, chunks // unroll)
    def _(block):
        for inner in range(unroll):
            index = block * unroll + inner
            at = pl.ds(pl.multiple_of(index * 8, 8), 8)
            put = pl.ds(pl.multiple_of(index * 8 + 8, 8), 8)
            after = pl.ds(pl.multiple_of(index * 8 + 16, 8), 8)
            here = source[put, :]
            above = jnp.where(row_mask == 0, pltpu.roll(source[at, :], 1, 0), pltpu.roll(here, 1, 0))
            below = jnp.where(row_mask == 7, pltpu.roll(source[after, :], 7, 0), pltpu.roll(here, 7, 0))
            dest[put, :] = (
                middle[at, :] * here
                + (north[at, :] * above + south[at, :] * below)
                + (
                    east[at, :] * pltpu.roll(here, length - 1, 1)
                    + west[at, :] * pltpu.roll(here, 1, 1)
                )
            )


def image_kernel(
    band_in, kern, ids, table, diff, target, diff_halo, target_halo, lh, ll, wh, wl, out,
    ah, al, mid, fields, coarse, field, other, east, west, north, south, middle,
    zh, zl, grad, qh, ql, th, tl, cells, goal, sems,
):
    count, _, band, _ = kern.shape
    rows, length = diff.shape
    total = rows + 2 * HALO
    points = 2 * band
    level = table[ids[0]]
    first = pl.multiple_of(lax.axis_index("slab") * rows, rows)
    row_mask = lax.broadcasted_iota(jnp.int32, (8, length), 0)
    chunks = total // 8
    coeffs = (east, west, north, south, middle)

    loads = [
        pltpu.make_async_copy(diff, cells.at[pl.ds(8 + HALO, rows)], sems.at[0]),
        pltpu.make_async_copy(diff_halo.at[0], cells.at[pl.ds(8, HALO)], sems.at[1]),
        pltpu.make_async_copy(diff_halo.at[1], cells.at[pl.ds(8 + HALO + rows, HALO)], sems.at[2]),
        pltpu.make_async_copy(target, goal.at[pl.ds(HALO, rows)], sems.at[3]),
        pltpu.make_async_copy(target_halo.at[0], goal.at[pl.ds(0, HALO)], sems.at[4]),
        pltpu.make_async_copy(target_halo.at[1], goal.at[pl.ds(HALO + rows, HALO)], sems.at[5]),
    ]
    for load in loads:
        load.start()
    blank = jnp.zeros((8, length), f32)
    for ref in (cells, field, other):
        ref[0:8, :] = blank
        ref[total + 8 : total + 16, :] = blank
    th[...] = lh[...].astype(f32).T.astype(bf16)
    tl[...] = ll[...].astype(f32).T.astype(bf16)

    real, imag = band_in[0:band, :], band_in[band:, :]
    for k in range(count):
        cols = slice(k * band, (k + 1) * band)
        kr, ki = kern[k, 0], kern[k, 1]
        ah[0:band, cols], al[0:band, cols] = halves(kr * real - ki * imag)
        ah[band:, cols], al[band:, cols] = halves(kr * imag + ki * real)

    @pl.loop(0, count // 2)
    def _(pair):
        at = pl.ds(pl.multiple_of(pair * points, points), points)
        mid[:, at] = dot3((lh[...], ll[...]), (ah[:, at], al[:, at]))

    coarse[...] = jnp.zeros_like(coarse)

    @pl.loop(0, count)
    def _(k):
        at = pl.ds(pl.multiple_of(k * band, band), band)
        block = jnp.concatenate([mid[0:points, at], mid[points:, at]], axis=1)
        value = dot3(halves(block), (th[...], tl[...])) * (1.0 / band)
        fields[k] = value
        re, im = value[:, :points], value[:, points:]
        coarse[...] += re * re + im * im

    near = pl.ds(first, total)
    zh[...], zl[...] = halves(
        dot3((wh[near, :], wl[near, :]), halves(coarse[...] * (level / count)))
    )
    wide = 256

    @pl.loop(0, length // wide)
    def _(step):
        at = pl.ds(pl.multiple_of(step * wide, wide), wide)
        src = pl.ds(pl.multiple_of(step * wide + HALO, HALO), wide)
        field[8 : 8 + total, at] = dot3((zh[...], zl[...]), (wh[src, :], wl[src, :]), NT)

    for load in loads:
        load.wait()

    @pl.loop(0, chunks)
    def _(index):
        at = pl.ds(pl.multiple_of(index * 8, 8), 8)
        put = pl.ds(pl.multiple_of(index * 8 + 8, 8), 8)
        after = pl.ds(pl.multiple_of(index * 8 + 16, 8), 8)
        here = cells[put, :]
        above = jnp.where(row_mask == 0, pltpu.roll(cells[at, :], 1, 0), pltpu.roll(here, 1, 0))
        below = jnp.where(row_mask == 7, pltpu.roll(cells[after, :], 7, 0), pltpu.roll(here, 7, 0))
        c_e = 0.5 * (here + pltpu.roll(here, length - 1, 1))
        c_w = 0.5 * (here + pltpu.roll(here, 1, 1))
        c_n = 0.5 * (here + above)
        c_s = 0.5 * (here + below)
        east[at, :] = c_e
        west[at, :] = c_w
        north[at, :] = c_n
        south[at, :] = c_s
        middle[at, :] = 1.0 - ((c_e + c_w) + (c_n + c_s))

    @pl.loop(0, 2)
    def _(bake):
        @pl.loop(0, STEPS // 2)
        def _(pair):
            bake_sweep(field, other, coeffs, row_mask)
            bake_sweep(other, field, coeffs, row_mask)

        @pl.when(bake == 0)
        def _():
            @pl.loop(0, chunks)
            def _(index):
                at = pl.ds(pl.multiple_of(index * 8, 8), 8)
                put = pl.ds(pl.multiple_of(index * 8 + 8, 8), 8)
                resist = jax.nn.sigmoid(steepness * (field[put, :] - threshold))
                field[put, :] = (
                    steepness * (resist - goal[at, :].astype(f32)) * resist * (1.0 - resist)
                )

    grad[...] = jnp.zeros_like(grad)

    @pl.loop(0, length // wide)
    def _(step):
        at = pl.ds(pl.multiple_of(step * wide, wide), wide)
        src = pl.ds(pl.multiple_of(step * wide + HALO, HALO), wide)
        grad[...] += dot3(
            halves(field[8 + HALO : 8 + HALO + rows, at]), (wh[src, :], wl[src, :])
        )

    inside = pl.ds(pl.multiple_of(first + HALO, HALO), rows)
    spread = dot3((wh[inside, :], wl[inside, :]), halves(grad[...]), TN)
    coarse[...] = spread * (2.0 * level / count / band)

    @pl.loop(0, count)
    def _(k):
        at = pl.ds(pl.multiple_of(k * band, band), band)
        weight = coarse[...]
        block = fields[k] * jnp.concatenate([weight, weight], axis=1)
        back = dot3(halves(block), (lh[...], ll[...]))
        qh[0:points, at], ql[0:points, at] = halves(back[:, :band])
        qh[points:, at], ql[points:, at] = halves(back[:, band:])

    @pl.loop(0, count // 2)
    def _(pair):
        at = pl.ds(pl.multiple_of(pair * points, points), points)
        mid[0:points, at] = dot3((th[...], tl[...]), (qh[:, at], ql[:, at]))

    sum_re = jnp.zeros((band, band), f32)
    sum_im = jnp.zeros((band, band), f32)
    for k in range(count):
        cols = slice(k * band, (k + 1) * band)
        kr, ki = kern[k, 0], kern[k, 1]
        gr, gi = mid[0:band, cols], mid[band:points, cols]
        sum_re += kr * gr + ki * gi
        sum_im += kr * gi - ki * gr
    out[0:band, :] = sum_re
    out[band:, :] = sum_im


def final_kernel(grad, trans, tab_h, tab_l, out, bh, bl):
    rows, length = trans.shape
    band = grad.shape[1]
    top, low = grad[0:band, :], grad[band:, :]
    matrix = jnp.concatenate(
        [jnp.concatenate([top, low], 1), jnp.concatenate([low, -top], 1)], 0
    )
    mine = pl.ds(pl.multiple_of(lax.axis_index("slab") * rows, rows), rows)
    bh[...], bl[...] = halves(
        dot3((tab_h[mine, :], tab_l[mine, :]), halves(matrix)) * (0.5 / length)
    )
    wide = 256

    @pl.loop(0, length // wide)
    def _(step):
        at = pl.ds(pl.multiple_of(step * wide, wide), wide)
        value = dot3((bh[...], bl[...]), (tab_h[at, :], tab_l[at, :]), NT)
        t = trans[:, at]
        out[:, at] = value * (1.0 - t * t)


def sum_kernel(axes, with_edges, *refs):
    if with_edges:
        part, diff, target, out, diff_halo, target_halo = refs[:6]
        refs = refs[6:]
        edge_send, edge_recv = refs[-2:]
        refs = refs[:-2]
    else:
        part, out = refs[:2]
        refs = refs[2:]
    if "cond" in axes:
        landed, send, recv, mine, crossed, cross_send, cross_recv = refs
    else:
        landed, send, recv = refs
    count = lax.axis_size("slab")
    me = lax.axis_index("slab")
    conds = lax.axis_size("cond")
    chunk = part.shape[0] // count
    peer = [lax.rem(me + d, count) for d in range(count)]
    rank = lax.axis_index("cond")

    barrier = pltpu.get_barrier_semaphore()
    for d in range(1, count):
        pl.semaphore_signal(barrier, inc=1, device_id={"slab": peer[d]}, device_id_type=MESH)
    waits = count - 1
    if "cond" in axes:
        for d in range(1, conds):
            pl.semaphore_signal(
                barrier, inc=1, device_id={"cond": lax.rem(rank + d, conds)}, device_id_type=MESH
            )
        waits += conds - 1
    pl.semaphore_wait(barrier, waits)

    def rows_of(owner):
        return pl.ds(pl.multiple_of(owner * chunk, chunk), chunk)

    first = [
        pltpu.make_async_remote_copy(
            src_ref=part.at[rows_of(peer[d])],
            dst_ref=landed.at[d],
            send_sem=send.at[0, d],
            recv_sem=recv.at[0, d],
            device_id={"slab": peer[d]},
            device_id_type=MESH,
        )
        for d in range(1, count)
    ]
    for copy in first:
        copy.start()
    edges = []
    if with_edges:
        rows = diff.shape[0]
        for number, (source, halo) in enumerate(((diff, diff_halo), (target, target_halo))):
            for side, start, to in ((0, rows - HALO, 1), (1, 0, count - 1)):
                at = 2 * number + side
                edges.append(
                    pltpu.make_async_remote_copy(
                        src_ref=source.at[pl.ds(start, HALO)],
                        dst_ref=halo.at[side],
                        send_sem=edge_send.at[at],
                        recv_sem=edge_recv.at[at],
                        device_id={"slab": peer[to]},
                        device_id_type=MESH,
                    )
                )
        for copy in edges:
            copy.start()
    total = part[rows_of(me), :]
    for d, copy in enumerate(first, 1):
        copy.wait()
        total = total + landed[d]
    if "cond" in axes:
        mine[...] = total
        cross = [
            pltpu.make_async_remote_copy(
                src_ref=mine,
                dst_ref=crossed.at[rank],
                send_sem=cross_send.at[d],
                recv_sem=cross_recv.at[d],
                device_id={"cond": lax.rem(rank + d, conds)},
                device_id_type=MESH,
            )
            for d in range(1, conds)
        ]
        for copy in cross:
            copy.start()
        crossed[rank] = total
        for copy in cross:
            copy.wait()
        total = crossed[0]
        for c in range(1, conds):
            total = total + crossed[c]
    out[rows_of(me), :] = total
    second = [
        pltpu.make_async_remote_copy(
            src_ref=out.at[rows_of(me)],
            dst_ref=out.at[rows_of(me)],
            send_sem=send.at[1, d],
            recv_sem=recv.at[1, d],
            device_id={"slab": peer[d]},
            device_id_type=MESH,
        )
        for d in range(1, count)
    ]
    for copy in second:
        copy.start()
    for copy in second + edges:
        copy.wait()


def summed(part, axes, edges=()):
    count = lax.axis_size("slab")
    conds = lax.axis_size("cond")
    chunk = part.shape[0] // count
    dma = pltpu.SemaphoreType.DMA
    scratch = [pltpu.VMEM((count, chunk, part.shape[1]), f32), dma((2, count)), dma((2, count))]
    if "cond" in axes:
        scratch += [
            pltpu.VMEM((chunk, part.shape[1]), f32),
            pltpu.VMEM((conds, chunk, part.shape[1]), f32),
            dma((conds,)),
            dma((conds,)),
        ]
    if edges:
        scratch += [dma((4,)), dma((4,))]
    return pl.pallas_call(
        functools.partial(sum_kernel, axes, bool(edges)),
        out_shape=(shape(part.shape),)
        + tuple(shape((2, HALO, e.shape[1]), e.dtype) for e in edges),
        in_specs=[VMEM] + [ANY] * len(edges),
        out_specs=(VMEM,) * (1 + len(edges)),
        scratch_shapes=scratch,
        compiler_params=pltpu.CompilerParams(
            collective_id=len(axes), has_side_effects=True
        ),
        name="sum_" + "_".join(axes),
    )(part, *edges)


def shape(dims, kind=f32):
    return jax.ShapeDtypeStruct(dims, kind)


def shards(mask_pixels, target_bits, perturb, diffusivity, kernels, cond_ids, dose_table):
    rows, length = mask_pixels.shape
    count, band = kernels.shape[1], kernels.shape[-1]
    points = 2 * band
    total = rows + 2 * HALO
    params = pltpu.CompilerParams(vmem_limit_bytes=60 * 1024 * 1024)
    small, large = angle_parts(length, band, 64)
    left = coarse_tables(band)
    lh, ll = split_np(left)
    wh, wl = split_np(interpolation_table(length, band))
    trans, tab_h, tab_l, local = pl.pallas_call(
        project_kernel,
        out_shape=(
            shape((rows, length)),
            shape((length, points), bf16),
            shape((length, points), bf16),
            shape((points, band)),
        ),
        in_specs=[VMEM] * 4,
        out_specs=(VMEM,) * 4,
        scratch_shapes=[pltpu.VMEM((rows, points), f32)],
        compiler_params=params,
        name="project",
    )(mask_pixels, perturb, small, large)
    mask_band, diff_halo, target_halo = summed(local, ("slab",), (diffusivity, target_bits))
    part = pl.pallas_call(
        image_kernel,
        out_shape=shape((points, band)),
        in_specs=[VMEM] * 2 + [SMEM] * 2 + [ANY] * 2 + [VMEM] * 6,
        out_specs=VMEM,
        scratch_shapes=[
            pltpu.VMEM((points, count * band), bf16),
            pltpu.VMEM((points, count * band), bf16),
            pltpu.VMEM((2 * points, count * band), f32),
            pltpu.VMEM((count, points, 2 * points), f32),
            pltpu.VMEM((points, points), f32),
            pltpu.VMEM((total + 16, length), f32),
            pltpu.VMEM((total + 16, length), f32),
            pltpu.VMEM((total, length), f32),
            pltpu.VMEM((total, length), f32),
            pltpu.VMEM((total, length), f32),
            pltpu.VMEM((total, length), f32),
            pltpu.VMEM((total, length), f32),
            pltpu.VMEM((total, points), bf16),
            pltpu.VMEM((total, points), bf16),
            pltpu.VMEM((rows, points), f32),
            pltpu.VMEM((2 * points, count * band), bf16),
            pltpu.VMEM((2 * points, count * band), bf16),
            pltpu.VMEM((points, 2 * points), bf16),
            pltpu.VMEM((points, 2 * points), bf16),
            pltpu.VMEM((total + 16, length), f32),
            pltpu.VMEM((total, length), jnp.int32),
            pltpu.SemaphoreType.DMA((6,)),
        ],
        compiler_params=params,
        name="image",
    )(
        mask_band, kernels[0], cond_ids, dose_table, diffusivity, target_bits,
        diff_halo, target_halo, lh, ll, wh, wl,
    )
    (grad,) = summed(part, ("cond", "slab"))
    return pl.pallas_call(
        final_kernel,
        out_shape=shape((rows, length)),
        in_specs=[VMEM] * 4,
        out_specs=VMEM,
        scratch_shapes=[
            pltpu.VMEM((rows, points), bf16),
            pltpu.VMEM((rows, points), bf16),
        ],
        compiler_params=params,
        name="final",
    )(grad, trans, tab_h, tab_l)


def solution(mesh):
    placed = (
        P("slab", None),
        P("slab", None),
        P("slab", None),
        P("slab", None),
        P("cond", None, None, None, None),
        P("cond"),
        P(),
    )
    return jax.shard_map(
        shards, mesh=mesh, in_specs=placed, out_specs=P("slab", None), check_vma=False
    )
```

```python
import functools
import math

import jax
import jax.numpy as jnp
import numpy as np
from jax import lax
from jax.experimental import pallas as pl
from jax.experimental.pallas import tpu as pltpu
from jax.sharding import PartitionSpec as P

STEPS = 4
HALO = 2 * STEPS

steepness = 4.0
threshold = 1.0
theta_scale = 2.5

f32 = jnp.float32
bf16 = jnp.bfloat16
VMEM = pl.BlockSpec(memory_space=pltpu.VMEM)
ANY = pl.BlockSpec(memory_space=pl.ANY)
MESH = pl.DeviceIdType.MESH
SMEM = pl.BlockSpec(memory_space=pltpu.SMEM)
NN = (((1,), (0,)), ((), ()))
NT = (((1,), (1,)), ((), ()))
TN = (((0,), (0,)), ((), ()))


def split_np(table):
    high = table.astype(bf16)
    low = (table - high.astype(np.float64)).astype(bf16)
    return jnp.asarray(high), jnp.asarray(low)


def coarse_tables(band):
    points = 2 * band
    turns = np.arange(points)[:, None] * (np.arange(band)[None, :] - band // 2) % points
    angle = turns * (2.0 * math.pi / points)
    cos, sin = np.cos(angle), np.sin(angle)
    return np.concatenate(
        [np.concatenate([cos, -sin], 1), np.concatenate([sin, cos], 1)], 0
    )


def interpolation_table(length, band):
    points = 2 * band
    fine = np.arange(-HALO, length + HALO)
    scale = length // points
    offset = (fine[:, None] - scale * np.arange(points)[None, :]) % length
    freq = np.arange(1, band)
    profile = 1.0 + 2.0 * np.cos(
        (np.arange(length)[:, None] * freq[None, :] % length) * (2.0 * math.pi / length)
    ).sum(1)
    return profile[offset] / points


def angle_parts(length, band, inner):
    freq = np.arange(band) - band // 2
    fine = (np.arange(inner)[:, None] * freq % length) * (2.0 * math.pi / length)
    jump = (np.arange(length // inner)[:, None] * inner * freq % length) * (
        2.0 * math.pi / length
    )
    small = np.stack([np.cos(fine), np.sin(fine)]).astype(np.float32)
    large = np.stack([np.cos(jump), np.sin(jump)]).astype(np.float32)
    return jnp.asarray(small), jnp.asarray(large)


def halves(value):
    high = value.astype(bf16)
    return high, (value - high.astype(f32)).astype(bf16)


def dot3(left, right, dims=NN):
    go = lambda a, b: lax.dot_general(a, b, dims, preferred_element_type=f32)
    return go(left[0], right[0]) + (go(left[0], right[1]) + go(left[1], right[0]))


def project_kernel(mask, perturb, small, large, trans, tab_h, tab_l, band_out, acc):
    rows, length = mask.shape
    band = small.shape[2]
    inner = small.shape[1]
    cos_b, sin_b = small[0], small[1]

    @pl.loop(0, length // inner)
    def _(step):
        cos_a = large[0, pl.ds(step, 1), :]
        sin_a = large[1, pl.ds(step, 1), :]
        at = pl.ds(pl.multiple_of(step * inner, inner), inner)
        for part, value in (
            (0, cos_a * cos_b - sin_a * sin_b),
            (1, -(sin_a * cos_b + cos_a * sin_b)),
        ):
            high, low = halves(value)
            tab_h[at, part * band : (part + 1) * band] = high
            tab_l[at, part * band : (part + 1) * band] = low

    acc[...] = jnp.zeros_like(acc)
    wide = 256

    @pl.loop(0, length // wide)
    def _(step):
        at = pl.ds(pl.multiple_of(step * wide, wide), wide)
        theta = theta_scale * (2.0 * mask[:, at].astype(f32) - 1.0) + perturb[:, at]
        value = jnp.tanh(0.5 * theta)
        trans[:, at] = value
        acc[...] += dot3(halves(value), (tab_h[at, :], tab_l[at, :]))

    mine = pl.ds(pl.multiple_of(lax.axis_index("slab") * rows, rows), rows)
    mixed = dot3((tab_h[mine, :], tab_l[mine, :]), halves(acc[...] / length), TN)
    band_out[0:band, :] = mixed[0:band, 0:band] - mixed[band:, band:]
    band_out[band:, :] = mixed[0:band, band:] + mixed[band:, 0:band]


def bake_sweep(source, dest, coeffs, row_mask):
    east, west, north, south, middle = coeffs
    total, length = middle.shape
    chunks = total // 8
    unroll = max(d for d in range(1, 18) if chunks % d == 0)

    @pl.loop(0, chunks // unroll)
    def _(block):
        for inner in range(unroll):
            index = block * unroll + inner
            at = pl.ds(pl.multiple_of(index * 8, 8), 8)
            put = pl.ds(pl.multiple_of(index * 8 + 8, 8), 8)
            after = pl.ds(pl.multiple_of(index * 8 + 16, 8), 8)
            here = source[put, :]
            above = jnp.where(row_mask == 0, pltpu.roll(source[at, :], 1, 0), pltpu.roll(here, 1, 0))
            below = jnp.where(row_mask == 7, pltpu.roll(source[after, :], 7, 0), pltpu.roll(here, 7, 0))
            dest[put, :] = (
                middle[at, :] * here
                + (north[at, :] * above + south[at, :] * below)
                + (
                    east[at, :] * pltpu.roll(here, length - 1, 1)
                    + west[at, :] * pltpu.roll(here, 1, 1)
                )
            )


def image_kernel(
    band_in, kern, ids, table, diff, target, diff_halo, target_halo, lh, ll, wh, wl, out,
    ah, al, mid, fields, coarse, field, other, east, west, north, south, middle,
    zh, zl, grad, qh, ql, th, tl, cells, goal, sems,
):
    count, _, band, _ = kern.shape
    rows, length = diff.shape
    total = rows + 2 * HALO
    points = 2 * band
    level = table[ids[0]]
    first = pl.multiple_of(lax.axis_index("slab") * rows, rows)
    row_mask = lax.broadcasted_iota(jnp.int32, (8, length), 0)
    chunks = total // 8
    coeffs = (east, west, north, south, middle)

    loads = [
        pltpu.make_async_copy(diff, cells.at[pl.ds(8 + HALO, rows)], sems.at[0]),
        pltpu.make_async_copy(diff_halo.at[0], cells.at[pl.ds(8, HALO)], sems.at[1]),
        pltpu.make_async_copy(diff_halo.at[1], cells.at[pl.ds(8 + HALO + rows, HALO)], sems.at[2]),
        pltpu.make_async_copy(target, goal.at[pl.ds(HALO, rows)], sems.at[3]),
        pltpu.make_async_copy(target_halo.at[0], goal.at[pl.ds(0, HALO)], sems.at[4]),
        pltpu.make_async_copy(target_halo.at[1], goal.at[pl.ds(HALO + rows, HALO)], sems.at[5]),
    ]
    for load in loads:
        load.start()
    blank = jnp.zeros((8, length), f32)
    for ref in (cells, field, other):
        ref[0:8, :] = blank
        ref[total + 8 : total + 16, :] = blank
    th[...] = lh[...].astype(f32).T.astype(bf16)
    tl[...] = ll[...].astype(f32).T.astype(bf16)

    real, imag = band_in[0:band, :], band_in[band:, :]
    for k in range(count):
        cols = slice(k * band, (k + 1) * band)
        kr, ki = kern[k, 0], kern[k, 1]
        ah[0:band, cols], al[0:band, cols] = halves(kr * real - ki * imag)
        ah[band:, cols], al[band:, cols] = halves(kr * imag + ki * real)

    @pl.loop(0, count // 2)
    def _(pair):
        at = pl.ds(pl.multiple_of(pair * points, points), points)
        mid[:, at] = dot3((lh[...], ll[...]), (ah[:, at], al[:, at]))

    coarse[...] = jnp.zeros_like(coarse)

    @pl.loop(0, count)
    def _(k):
        at = pl.ds(pl.multiple_of(k * band, band), band)
        block = jnp.concatenate([mid[0:points, at], mid[points:, at]], axis=1)
        value = dot3(halves(block), (th[...], tl[...])) * (1.0 / band)
        fields[k] = value
        re, im = value[:, :points], value[:, points:]
        coarse[...] += re * re + im * im

    near = pl.ds(first, total)
    zh[...], zl[...] = halves(
        dot3((wh[near, :], wl[near, :]), halves(coarse[...] * (level / count)))
    )
    wide = 256

    @pl.loop(0, length // wide)
    def _(step):
        at = pl.ds(pl.multiple_of(step * wide, wide), wide)
        src = pl.ds(pl.multiple_of(step * wide + HALO, HALO), wide)
        field[8 : 8 + total, at] = dot3((zh[...], zl[...]), (wh[src, :], wl[src, :]), NT)

    for load in loads:
        load.wait()

    @pl.loop(0, chunks)
    def _(index):
        at = pl.ds(pl.multiple_of(index * 8, 8), 8)
        put = pl.ds(pl.multiple_of(index * 8 + 8, 8), 8)
        after = pl.ds(pl.multiple_of(index * 8 + 16, 8), 8)
        here = cells[put, :]
        above = jnp.where(row_mask == 0, pltpu.roll(cells[at, :], 1, 0), pltpu.roll(here, 1, 0))
        below = jnp.where(row_mask == 7, pltpu.roll(cells[after, :], 7, 0), pltpu.roll(here, 7, 0))
        c_e = 0.5 * (here + pltpu.roll(here, length - 1, 1))
        c_w = 0.5 * (here + pltpu.roll(here, 1, 1))
        c_n = 0.5 * (here + above)
        c_s = 0.5 * (here + below)
        east[at, :] = c_e
        west[at, :] = c_w
        north[at, :] = c_n
        south[at, :] = c_s
        middle[at, :] = 1.0 - ((c_e + c_w) + (c_n + c_s))

    @pl.loop(0, 2)
    def _(bake):
        @pl.loop(0, STEPS // 2)
        def _(pair):
            bake_sweep(field, other, coeffs, row_mask)
            bake_sweep(other, field, coeffs, row_mask)

        @pl.when(bake == 0)
        def _():
            @pl.loop(0, chunks)
            def _(index):
                at = pl.ds(pl.multiple_of(index * 8, 8), 8)
                put = pl.ds(pl.multiple_of(index * 8 + 8, 8), 8)
                resist = jax.nn.sigmoid(steepness * (field[put, :] - threshold))
                field[put, :] = (
                    steepness * (resist - goal[at, :].astype(f32)) * resist * (1.0 - resist)
                )

    grad[...] = jnp.zeros_like(grad)

    @pl.loop(0, length // wide)
    def _(step):
        at = pl.ds(pl.multiple_of(step * wide, wide), wide)
        src = pl.ds(pl.multiple_of(step * wide + HALO, HALO), wide)
        grad[...] += dot3(
            halves(field[8 + HALO : 8 + HALO + rows, at]), (wh[src, :], wl[src, :])
        )

    inside = pl.ds(pl.multiple_of(first + HALO, HALO), rows)
    spread = dot3((wh[inside, :], wl[inside, :]), halves(grad[...]), TN)
    coarse[...] = spread * (2.0 * level / count / band)

    @pl.loop(0, count)
    def _(k):
        at = pl.ds(pl.multiple_of(k * band, band), band)
        weight = coarse[...]
        block = fields[k] * jnp.concatenate([weight, weight], axis=1)
        back = dot3(halves(block), (lh[...], ll[...]))
        qh[0:points, at], ql[0:points, at] = halves(back[:, :band])
        qh[points:, at], ql[points:, at] = halves(back[:, band:])

    @pl.loop(0, count // 2)
    def _(pair):
        at = pl.ds(pl.multiple_of(pair * points, points), points)
        mid[0:points, at] = dot3((th[...], tl[...]), (qh[:, at], ql[:, at]))

    sum_re = jnp.zeros((band, band), f32)
    sum_im = jnp.zeros((band, band), f32)
    for k in range(count):
        cols = slice(k * band, (k + 1) * band)
        kr, ki = kern[k, 0], kern[k, 1]
        gr, gi = mid[0:band, cols], mid[band:points, cols]
        sum_re += kr * gr + ki * gi
        sum_im += kr * gi - ki * gr
    out[0:band, :] = sum_re
    out[band:, :] = sum_im


def final_kernel(grad, trans, tab_h, tab_l, out, bh, bl):
    rows, length = trans.shape
    band = grad.shape[1]
    top, low = grad[0:band, :], grad[band:, :]
    matrix = jnp.concatenate(
        [jnp.concatenate([top, low], 1), jnp.concatenate([low, -top], 1)], 0
    )
    mine = pl.ds(pl.multiple_of(lax.axis_index("slab") * rows, rows), rows)
    bh[...], bl[...] = halves(
        dot3((tab_h[mine, :], tab_l[mine, :]), halves(matrix)) * (0.5 / length)
    )
    wide = 256

    @pl.loop(0, length // wide)
    def _(step):
        at = pl.ds(pl.multiple_of(step * wide, wide), wide)
        value = dot3((bh[...], bl[...]), (tab_h[at, :], tab_l[at, :]), NT)
        t = trans[:, at]
        out[:, at] = value * (1.0 - t * t)


def sum_kernel(axes, with_edges, *refs):
    if with_edges:
        part, diff, target, out, diff_halo, target_halo = refs[:6]
        refs = refs[6:]
        edge_send, edge_recv = refs[-2:]
        refs = refs[:-2]
    else:
        part, out = refs[:2]
        refs = refs[2:]
    if "cond" in axes:
        landed, send, recv, mine, crossed, cross_send, cross_recv = refs
    else:
        landed, send, recv = refs
    count = lax.axis_size("slab")
    me = lax.axis_index("slab")
    conds = lax.axis_size("cond")
    chunk = part.shape[0] // count
    peer = [lax.rem(me + d, count) for d in range(count)]
    rank = lax.axis_index("cond")

    barrier = pltpu.get_barrier_semaphore()
    for d in range(1, count):
        pl.semaphore_signal(barrier, inc=1, device_id={"slab": peer[d]}, device_id_type=MESH)
    waits = count - 1
    if "cond" in axes:
        for d in range(1, conds):
            pl.semaphore_signal(
                barrier, inc=1, device_id={"cond": lax.rem(rank + d, conds)}, device_id_type=MESH
            )
        waits += conds - 1
    pl.semaphore_wait(barrier, waits)

    def rows_of(owner):
        return pl.ds(pl.multiple_of(owner * chunk, chunk), chunk)

    first = [
        pltpu.make_async_remote_copy(
            src_ref=part.at[rows_of(peer[d])],
            dst_ref=landed.at[d],
            send_sem=send.at[0, d],
            recv_sem=recv.at[0, d],
            device_id={"slab": peer[d]},
            device_id_type=MESH,
        )
        for d in range(1, count)
    ]
    for copy in first:
        copy.start()
    edges = []
    if with_edges:
        rows = diff.shape[0]
        for number, (source, halo) in enumerate(((diff, diff_halo), (target, target_halo))):
            for side, start, to in ((0, rows - HALO, 1), (1, 0, count - 1)):
                at = 2 * number + side
                edges.append(
                    pltpu.make_async_remote_copy(
                        src_ref=source.at[pl.ds(start, HALO)],
                        dst_ref=halo.at[side],
                        send_sem=edge_send.at[at],
                        recv_sem=edge_recv.at[at],
                        device_id={"slab": peer[to]},
                        device_id_type=MESH,
                    )
                )
        for copy in edges:
            copy.start()
    total = part[rows_of(me), :]
    for d, copy in enumerate(first, 1):
        copy.wait()
        total = total + landed[d]
    if "cond" in axes:
        mine[...] = total
        cross = [
            pltpu.make_async_remote_copy(
                src_ref=mine,
                dst_ref=crossed.at[rank],
                send_sem=cross_send.at[d],
                recv_sem=cross_recv.at[d],
                device_id={"cond": lax.rem(rank + d, conds)},
                device_id_type=MESH,
            )
            for d in range(1, conds)
        ]
        for copy in cross:
            copy.start()
        crossed[rank] = total
        for copy in cross:
            copy.wait()
        total = crossed[0]
        for c in range(1, conds):
            total = total + crossed[c]
    out[rows_of(me), :] = total
    second = [
        pltpu.make_async_remote_copy(
            src_ref=out.at[rows_of(me)],
            dst_ref=out.at[rows_of(me)],
            send_sem=send.at[1, d],
            recv_sem=recv.at[1, d],
            device_id={"slab": peer[d]},
            device_id_type=MESH,
        )
        for d in range(1, count)
    ]
    for copy in second:
        copy.start()
    for copy in second + edges:
        copy.wait()


def summed(part, axes, edges=()):
    count = lax.axis_size("slab")
    conds = lax.axis_size("cond")
    chunk = part.shape[0] // count
    dma = pltpu.SemaphoreType.DMA
    scratch = [pltpu.VMEM((count, chunk, part.shape[1]), f32), dma((2, count)), dma((2, count))]
    if "cond" in axes:
        scratch += [
            pltpu.VMEM((chunk, part.shape[1]), f32),
            pltpu.VMEM((conds, chunk, part.shape[1]), f32),
            dma((conds,)),
            dma((conds,)),
        ]
    if edges:
        scratch += [dma((4,)), dma((4,))]
    return pl.pallas_call(
        functools.partial(sum_kernel, axes, bool(edges)),
        out_shape=(shape(part.shape),)
        + tuple(shape((2, HALO, e.shape[1]), e.dtype) for e in edges),
        in_specs=[VMEM] + [ANY] * len(edges),
        out_specs=(VMEM,) * (1 + len(edges)),
        scratch_shapes=scratch,
        compiler_params=pltpu.CompilerParams(
            collective_id=len(axes), has_side_effects=True, vmem_limit_bytes=4 * 1024 * 1024
        ),
        name="sum_" + "_".join(axes),
    )(part, *edges)


def shape(dims, kind=f32):
    return jax.ShapeDtypeStruct(dims, kind)


def shards(mask_pixels, target_bits, perturb, diffusivity, kernels, cond_ids, dose_table):
    rows, length = mask_pixels.shape
    count, band = kernels.shape[1], kernels.shape[-1]
    points = 2 * band
    total = rows + 2 * HALO
    mib = 1024 * 1024
    params = pltpu.CompilerParams(vmem_limit_bytes=12 * mib)
    small, large = angle_parts(length, band, 64)
    left = coarse_tables(band)
    lh, ll = split_np(left)
    wh, wl = split_np(interpolation_table(length, band))
    trans, tab_h, tab_l, local = pl.pallas_call(
        project_kernel,
        out_shape=(
            shape((rows, length)),
            shape((length, points), bf16),
            shape((length, points), bf16),
            shape((points, band)),
        ),
        in_specs=[VMEM] * 4,
        out_specs=(VMEM,) * 4,
        scratch_shapes=[pltpu.VMEM((rows, points), f32)],
        compiler_params=params,
        name="project",
    )(mask_pixels, perturb, small, large)
    mask_band, diff_halo, target_halo = summed(local, ("slab",), (diffusivity, target_bits))
    part = pl.pallas_call(
        image_kernel,
        out_shape=shape((points, band)),
        in_specs=[VMEM] * 2 + [SMEM] * 2 + [ANY] * 2 + [VMEM] * 6,
        out_specs=VMEM,
        scratch_shapes=[
            pltpu.VMEM((points, count * band), bf16),
            pltpu.VMEM((points, count * band), bf16),
            pltpu.VMEM((2 * points, count * band), f32),
            pltpu.VMEM((count, points, 2 * points), f32),
            pltpu.VMEM((points, points), f32),
            pltpu.VMEM((total + 16, length), f32),
            pltpu.VMEM((total + 16, length), f32),
            pltpu.VMEM((total, length), f32),
            pltpu.VMEM((total, length), f32),
            pltpu.VMEM((total, length), f32),
            pltpu.VMEM((total, length), f32),
            pltpu.VMEM((total, length), f32),
            pltpu.VMEM((total, points), bf16),
            pltpu.VMEM((total, points), bf16),
            pltpu.VMEM((rows, points), f32),
            pltpu.VMEM((2 * points, count * band), bf16),
            pltpu.VMEM((2 * points, count * band), bf16),
            pltpu.VMEM((points, 2 * points), bf16),
            pltpu.VMEM((points, 2 * points), bf16),
            pltpu.VMEM((total + 16, length), f32),
            pltpu.VMEM((total, length), jnp.int32),
            pltpu.SemaphoreType.DMA((6,)),
        ],
        compiler_params=pltpu.CompilerParams(vmem_limit_bytes=40 * mib),
        name="image",
    )(
        mask_band, kernels[0], cond_ids, dose_table, diffusivity, target_bits,
        diff_halo, target_halo, lh, ll, wh, wl,
    )
    (grad,) = summed(part, ("cond", "slab"))
    return pl.pallas_call(
        final_kernel,
        out_shape=shape((rows, length)),
        in_specs=[VMEM] * 4,
        out_specs=VMEM,
        scratch_shapes=[
            pltpu.VMEM((rows, points), bf16),
            pltpu.VMEM((rows, points), bf16),
        ],
        compiler_params=params,
        name="final",
    )(grad, trans, tab_h, tab_l)


def solution(mesh):
    placed = (
        P("slab", None),
        P("slab", None),
        P("slab", None),
        P("slab", None),
        P("cond", None, None, None, None),
        P("cond"),
        P(),
    )
    return jax.shard_map(
        shards, mesh=mesh, in_specs=placed, out_specs=P("slab", None), check_vma=False
    )
```

```python
import functools
import math

import jax
import jax.numpy as jnp
import numpy as np
from jax import lax
from jax.experimental import pallas as pl
from jax.experimental.pallas import tpu as pltpu
from jax.sharding import PartitionSpec as P

STEPS = 4
HALO = 2 * STEPS

steepness = 4.0
threshold = 1.0
theta_scale = 2.5

f32 = jnp.float32
bf16 = jnp.bfloat16
VMEM = pl.BlockSpec(memory_space=pltpu.VMEM)
ANY = pl.BlockSpec(memory_space=pl.ANY)
MESH = pl.DeviceIdType.MESH
SMEM = pl.BlockSpec(memory_space=pltpu.SMEM)
NN = (((1,), (0,)), ((), ()))
NT = (((1,), (1,)), ((), ()))
TN = (((0,), (0,)), ((), ()))


def split_np(table):
    high = table.astype(bf16)
    low = (table - high.astype(np.float64)).astype(bf16)
    return jnp.asarray(high), jnp.asarray(low)


def coarse_tables(band):
    points = 2 * band
    turns = np.arange(points)[:, None] * (np.arange(band)[None, :] - band // 2) % points
    angle = turns * (2.0 * math.pi / points)
    cos, sin = np.cos(angle), np.sin(angle)
    return np.concatenate(
        [np.concatenate([cos, -sin], 1), np.concatenate([sin, cos], 1)], 0
    )


def interpolation_table(length, band):
    points = 2 * band
    fine = np.arange(-HALO, length + HALO)
    scale = length // points
    offset = (fine[:, None] - scale * np.arange(points)[None, :]) % length
    freq = np.arange(1, band)
    profile = 1.0 + 2.0 * np.cos(
        (np.arange(length)[:, None] * freq[None, :] % length) * (2.0 * math.pi / length)
    ).sum(1)
    return profile[offset] / points


def angle_parts(length, band, inner):
    freq = np.arange(band) - band // 2
    fine = (np.arange(inner)[:, None] * freq % length) * (2.0 * math.pi / length)
    jump = (np.arange(length // inner)[:, None] * inner * freq % length) * (
        2.0 * math.pi / length
    )
    small = np.stack([np.cos(fine), np.sin(fine)]).astype(np.float32)
    large = np.stack([np.cos(jump), np.sin(jump)]).astype(np.float32)
    return jnp.asarray(small), jnp.asarray(large)


def halves(value):
    high = value.astype(bf16)
    return high, (value - high.astype(f32)).astype(bf16)


def dot3(left, right, dims=NN):
    go = lambda a, b: lax.dot_general(a, b, dims, preferred_element_type=f32)
    return go(left[0], right[0]) + (go(left[0], right[1]) + go(left[1], right[0]))


def project_kernel(mask, perturb, small, large, trans, tab_h, tab_l, band_out, acc):
    rows, length = mask.shape
    band = small.shape[2]
    inner = small.shape[1]
    cos_b, sin_b = small[0], small[1]

    @pl.loop(0, length // inner)
    def _(step):
        cos_a = large[0, pl.ds(step, 1), :]
        sin_a = large[1, pl.ds(step, 1), :]
        at = pl.ds(pl.multiple_of(step * inner, inner), inner)
        for part, value in (
            (0, cos_a * cos_b - sin_a * sin_b),
            (1, -(sin_a * cos_b + cos_a * sin_b)),
        ):
            high, low = halves(value)
            tab_h[at, part * band : (part + 1) * band] = high
            tab_l[at, part * band : (part + 1) * band] = low

    acc[...] = jnp.zeros_like(acc)
    wide = 256

    @pl.loop(0, length // wide)
    def _(step):
        at = pl.ds(pl.multiple_of(step * wide, wide), wide)
        theta = theta_scale * (2.0 * mask[:, at].astype(f32) - 1.0) + perturb[:, at]
        value = jnp.tanh(0.5 * theta)
        trans[:, at] = value
        acc[...] += dot3(halves(value), (tab_h[at, :], tab_l[at, :]))

    mine = pl.ds(pl.multiple_of(lax.axis_index("slab") * rows, rows), rows)
    mixed = dot3((tab_h[mine, :], tab_l[mine, :]), halves(acc[...] / length), TN)
    band_out[0:band, :] = mixed[0:band, 0:band] - mixed[band:, band:]
    band_out[band:, :] = mixed[0:band, band:] + mixed[band:, 0:band]


def bake_sweep(source, dest, coeffs, row_mask):
    east, west, north, south, middle = coeffs
    total, length = middle.shape
    chunks = total // 8
    unroll = max(d for d in range(1, 18) if chunks % d == 0)

    @pl.loop(0, chunks // unroll)
    def _(block):
        for inner in range(unroll):
            index = block * unroll + inner
            at = pl.ds(pl.multiple_of(index * 8, 8), 8)
            put = pl.ds(pl.multiple_of(index * 8 + 8, 8), 8)
            after = pl.ds(pl.multiple_of(index * 8 + 16, 8), 8)
            here = source[put, :]
            above = jnp.where(row_mask == 0, pltpu.roll(source[at, :], 1, 0), pltpu.roll(here, 1, 0))
            below = jnp.where(row_mask == 7, pltpu.roll(source[after, :], 7, 0), pltpu.roll(here, 7, 0))
            dest[put, :] = (
                middle[at, :] * here
                + (north[at, :] * above + south[at, :] * below)
                + (
                    east[at, :] * pltpu.roll(here, length - 1, 1)
                    + west[at, :] * pltpu.roll(here, 1, 1)
                )
            )


def image_kernel(
    band_in, kern, ids, table, diff, target, diff_halo, target_halo, lh, ll, wh, wl, out,
    ah, al, mid, fields, coarse, field, other, east, west, north, south, middle,
    zh, zl, grad, qh, ql, th, tl, cells, goal, sems,
):
    count, _, band, _ = kern.shape
    rows, length = diff.shape
    total = rows + 2 * HALO
    points = 2 * band
    level = table[ids[0]]
    first = pl.multiple_of(lax.axis_index("slab") * rows, rows)
    row_mask = lax.broadcasted_iota(jnp.int32, (8, length), 0)
    chunks = total // 8
    coeffs = (east, west, north, south, middle)

    loads = [
        pltpu.make_async_copy(diff, cells.at[pl.ds(8 + HALO, rows)], sems.at[0]),
        pltpu.make_async_copy(diff_halo.at[0], cells.at[pl.ds(8, HALO)], sems.at[1]),
        pltpu.make_async_copy(diff_halo.at[1], cells.at[pl.ds(8 + HALO + rows, HALO)], sems.at[2]),
        pltpu.make_async_copy(target, goal.at[pl.ds(HALO, rows)], sems.at[3]),
        pltpu.make_async_copy(target_halo.at[0], goal.at[pl.ds(0, HALO)], sems.at[4]),
        pltpu.make_async_copy(target_halo.at[1], goal.at[pl.ds(HALO + rows, HALO)], sems.at[5]),
    ]
    for load in loads:
        load.start()
    blank = jnp.zeros((8, length), f32)
    for ref in (cells, field, other):
        ref[0:8, :] = blank
        ref[total + 8 : total + 16, :] = blank
    th[...] = lh[...].astype(f32).T.astype(bf16)
    tl[...] = ll[...].astype(f32).T.astype(bf16)

    real, imag = band_in[0:band, :], band_in[band:, :]
    for k in range(count):
        cols = slice(k * band, (k + 1) * band)
        kr, ki = kern[k, 0], kern[k, 1]
        ah[0:band, cols], al[0:band, cols] = halves(kr * real - ki * imag)
        ah[band:, cols], al[band:, cols] = halves(kr * imag + ki * real)

    @pl.loop(0, count // 2)
    def _(pair):
        at = pl.ds(pl.multiple_of(pair * points, points), points)
        mid[:, at] = dot3((lh[...], ll[...]), (ah[:, at], al[:, at]))

    coarse[...] = jnp.zeros_like(coarse)

    @pl.loop(0, count)
    def _(k):
        at = pl.ds(pl.multiple_of(k * band, band), band)
        block = jnp.concatenate([mid[0:points, at], mid[points:, at]], axis=1)
        value = dot3(halves(block), (th[...], tl[...])) * (1.0 / band)
        fields[k] = value
        re, im = value[:, :points], value[:, points:]
        coarse[...] += re * re + im * im

    near = pl.ds(first, total)
    zh[...], zl[...] = halves(
        dot3((wh[near, :], wl[near, :]), halves(coarse[...] * (level / count)))
    )
    wide = 256

    @pl.loop(0, length // wide)
    def _(step):
        at = pl.ds(pl.multiple_of(step * wide, wide), wide)
        src = pl.ds(pl.multiple_of(step * wide + HALO, HALO), wide)
        field[8 : 8 + total, at] = dot3((zh[...], zl[...]), (wh[src, :], wl[src, :]), NT)

    for load in loads:
        load.wait()

    @pl.loop(0, chunks)
    def _(index):
        at = pl.ds(pl.multiple_of(index * 8, 8), 8)
        put = pl.ds(pl.multiple_of(index * 8 + 8, 8), 8)
        after = pl.ds(pl.multiple_of(index * 8 + 16, 8), 8)
        here = cells[put, :]
        above = jnp.where(row_mask == 0, pltpu.roll(cells[at, :], 1, 0), pltpu.roll(here, 1, 0))
        below = jnp.where(row_mask == 7, pltpu.roll(cells[after, :], 7, 0), pltpu.roll(here, 7, 0))
        c_e = 0.5 * (here + pltpu.roll(here, length - 1, 1))
        c_w = 0.5 * (here + pltpu.roll(here, 1, 1))
        c_n = 0.5 * (here + above)
        c_s = 0.5 * (here + below)
        east[at, :] = c_e
        west[at, :] = c_w
        north[at, :] = c_n
        south[at, :] = c_s
        middle[at, :] = 1.0 - ((c_e + c_w) + (c_n + c_s))

    @pl.loop(0, 2)
    def _(bake):
        @pl.loop(0, STEPS // 2)
        def _(pair):
            bake_sweep(field, other, coeffs, row_mask)
            bake_sweep(other, field, coeffs, row_mask)

        @pl.when(bake == 0)
        def _():
            @pl.loop(0, chunks)
            def _(index):
                at = pl.ds(pl.multiple_of(index * 8, 8), 8)
                put = pl.ds(pl.multiple_of(index * 8 + 8, 8), 8)
                resist = jax.nn.sigmoid(steepness * (field[put, :] - threshold))
                field[put, :] = (
                    steepness * (resist - goal[at, :].astype(f32)) * resist * (1.0 - resist)
                )

    grad[...] = jnp.zeros_like(grad)

    @pl.loop(0, length // wide)
    def _(step):
        at = pl.ds(pl.multiple_of(step * wide, wide), wide)
        src = pl.ds(pl.multiple_of(step * wide + HALO, HALO), wide)
        grad[...] += dot3(
            halves(field[8 + HALO : 8 + HALO + rows, at]), (wh[src, :], wl[src, :])
        )

    inside = pl.ds(pl.multiple_of(first + HALO, HALO), rows)
    spread = dot3((wh[inside, :], wl[inside, :]), halves(grad[...]), TN)
    coarse[...] = spread * (2.0 * level / count / band)

    @pl.loop(0, count)
    def _(k):
        at = pl.ds(pl.multiple_of(k * band, band), band)
        weight = coarse[...]
        block = fields[k] * jnp.concatenate([weight, weight], axis=1)
        back = dot3(halves(block), (lh[...], ll[...]))
        qh[0:points, at], ql[0:points, at] = halves(back[:, :band])
        qh[points:, at], ql[points:, at] = halves(back[:, band:])

    @pl.loop(0, count // 2)
    def _(pair):
        at = pl.ds(pl.multiple_of(pair * points, points), points)
        mid[0:points, at] = dot3((th[...], tl[...]), (qh[:, at], ql[:, at]))

    sum_re = jnp.zeros((band, band), f32)
    sum_im = jnp.zeros((band, band), f32)
    for k in range(count):
        cols = slice(k * band, (k + 1) * band)
        kr, ki = kern[k, 0], kern[k, 1]
        gr, gi = mid[0:band, cols], mid[band:points, cols]
        sum_re += kr * gr + ki * gi
        sum_im += kr * gi - ki * gr
    out[0:band, :] = sum_re
    out[band:, :] = sum_im


def final_kernel(grad, trans, tab_h, tab_l, out, bh, bl):
    rows, length = trans.shape
    band = grad.shape[1]
    top, low = grad[0:band, :], grad[band:, :]
    matrix = jnp.concatenate(
        [jnp.concatenate([top, low], 1), jnp.concatenate([low, -top], 1)], 0
    )
    mine = pl.ds(pl.multiple_of(lax.axis_index("slab") * rows, rows), rows)
    bh[...], bl[...] = halves(
        dot3((tab_h[mine, :], tab_l[mine, :]), halves(matrix)) * (0.5 / length)
    )
    wide = 256

    @pl.loop(0, length // wide)
    def _(step):
        at = pl.ds(pl.multiple_of(step * wide, wide), wide)
        value = dot3((bh[...], bl[...]), (tab_h[at, :], tab_l[at, :]), NT)
        t = trans[:, at]
        out[:, at] = value * (1.0 - t * t)


def sum_kernel(axes, with_edges, *refs):
    if with_edges:
        part, diff, target, out, diff_halo, target_halo = refs[:6]
        refs = refs[6:]
        edge_send, edge_recv = refs[-2:]
        refs = refs[:-2]
    else:
        part, out = refs[:2]
        refs = refs[2:]
    if "cond" in axes:
        landed, send, recv, mine, crossed, cross_send, cross_recv = refs
    else:
        landed, send, recv = refs
    count = lax.axis_size("slab")
    me = lax.axis_index("slab")
    conds = lax.axis_size("cond")
    chunk = part.shape[0] // count
    peer = [lax.rem(me + d, count) for d in range(count)]
    rank = lax.axis_index("cond")

    barrier = pltpu.get_barrier_semaphore()
    for d in range(1, count):
        pl.semaphore_signal(barrier, inc=1, device_id={"slab": peer[d]}, device_id_type=MESH)
    waits = count - 1
    if "cond" in axes:
        for d in range(1, conds):
            pl.semaphore_signal(
                barrier, inc=1, device_id={"cond": lax.rem(rank + d, conds)}, device_id_type=MESH
            )
        waits += conds - 1
    pl.semaphore_wait(barrier, waits)

    def rows_of(owner):
        return pl.ds(pl.multiple_of(owner * chunk, chunk), chunk)

    first = [
        pltpu.make_async_remote_copy(
            src_ref=part.at[rows_of(peer[d])],
            dst_ref=landed.at[d],
            send_sem=send.at[0, d],
            recv_sem=recv.at[0, d],
            device_id={"slab": peer[d]},
            device_id_type=MESH,
        )
        for d in range(1, count)
    ]
    for copy in first:
        copy.start()
    edges = []
    if with_edges:
        rows = diff.shape[0]
        for number, (source, halo) in enumerate(((diff, diff_halo), (target, target_halo))):
            for side, start, to in ((0, rows - HALO, 1), (1, 0, count - 1)):
                at = 2 * number + side
                edges.append(
                    pltpu.make_async_remote_copy(
                        src_ref=source.at[pl.ds(start, HALO)],
                        dst_ref=halo.at[side],
                        send_sem=edge_send.at[at],
                        recv_sem=edge_recv.at[at],
                        device_id={"slab": peer[to]},
                        device_id_type=MESH,
                    )
                )
        for copy in edges:
            copy.start()
    total = part[rows_of(me), :]
    for d, copy in enumerate(first, 1):
        copy.wait()
        total = total + landed[d]
    if "cond" in axes:
        mine[...] = total
        cross = [
            pltpu.make_async_remote_copy(
                src_ref=mine,
                dst_ref=crossed.at[rank],
                send_sem=cross_send.at[d],
                recv_sem=cross_recv.at[d],
                device_id={"cond": lax.rem(rank + d, conds)},
                device_id_type=MESH,
            )
            for d in range(1, conds)
        ]
        for copy in cross:
            copy.start()
        crossed[rank] = total
        for copy in cross:
            copy.wait()
        total = crossed[0]
        for c in range(1, conds):
            total = total + crossed[c]
    out[rows_of(me), :] = total
    second = [
        pltpu.make_async_remote_copy(
            src_ref=out.at[rows_of(me)],
            dst_ref=out.at[rows_of(me)],
            send_sem=send.at[1, d],
            recv_sem=recv.at[1, d],
            device_id={"slab": peer[d]},
            device_id_type=MESH,
        )
        for d in range(1, count)
    ]
    for copy in second:
        copy.start()
    for copy in second + edges:
        copy.wait()


def flat_kernel(axes, with_edges, *refs):
    if with_edges:
        part, diff, target, out, diff_halo, target_halo, landed, send, recv, edge_send, edge_recv = refs
    else:
        part, out, landed, send, recv = refs
    count = lax.axis_size("slab")
    conds = lax.axis_size("cond")
    me = lax.axis_index("slab")
    rank = lax.axis_index("cond")
    chunk = part.shape[0] // (count * conds)
    peer = [lax.rem(me + d, count) for d in range(count)]
    others = [(c, d) for c in range(conds) for d in range(count) if c or d]

    def place(c, d):
        return {"cond": lax.rem(rank + c, conds), "slab": lax.rem(me + d, count)}

    def rows_of(where):
        owner = where["slab"] * conds + where["cond"]
        return pl.ds(pl.multiple_of(owner * chunk, chunk), chunk)

    barrier = pltpu.get_barrier_semaphore()
    for c, d in others:
        pl.semaphore_signal(barrier, inc=1, device_id=place(c, d), device_id_type=MESH)
    pl.semaphore_wait(barrier, len(others))

    adders = others if "cond" in axes else [(c, d) for c, d in others if c == 0]
    first = []
    for c, d in adders:
        first.append(
            pltpu.make_async_remote_copy(
                src_ref=part.at[rows_of(place(c, d))],
                dst_ref=landed.at[c * count + d],
                send_sem=send.at[0, c * count + d],
                recv_sem=recv.at[0, c * count + d],
                device_id=place(c, d),
                device_id_type=MESH,
            )
        )
    for copy in first:
        copy.start()
    edges = []
    if with_edges:
        rows = diff.shape[0]
        for number, (source, halo) in enumerate(((diff, diff_halo), (target, target_halo))):
            for side, start, to in ((0, rows - HALO, 1), (1, 0, count - 1)):
                at = 2 * number + side
                edges.append(
                    pltpu.make_async_remote_copy(
                        src_ref=source.at[pl.ds(start, HALO)],
                        dst_ref=halo.at[side],
                        send_sem=edge_send.at[at],
                        recv_sem=edge_recv.at[at],
                        device_id={"slab": peer[to]},
                        device_id_type=MESH,
                    )
                )
        for copy in edges:
            copy.start()
    mine = rows_of(place(0, 0))
    total = part[mine, :]
    for (c, d), copy in zip(adders, first):
        copy.wait()
        total = total + landed[c * count + d]
    out[mine, :] = total
    second = [
        pltpu.make_async_remote_copy(
            src_ref=out.at[mine],
            dst_ref=out.at[mine],
            send_sem=send.at[1, c * count + d],
            recv_sem=recv.at[1, c * count + d],
            device_id=place(c, d),
            device_id_type=MESH,
        )
        for c, d in others
    ]
    for copy in second:
        copy.start()
    for copy in second + edges:
        copy.wait()


def summed(part, axes, edges=()):
    count = lax.axis_size("slab")
    conds = lax.axis_size("cond")
    chunk = part.shape[0] // count
    dma = pltpu.SemaphoreType.DMA
    scratch = [pltpu.VMEM((count, chunk, part.shape[1]), f32), dma((2, count)), dma((2, count))]
    flat = part.shape[0] % (8 * count * conds) == 0
    if flat:
        owners = count * conds
        scratch = [
            pltpu.VMEM((owners, part.shape[0] // owners, part.shape[1]), f32),
            dma((2, owners)),
            dma((2, owners)),
        ]
    elif "cond" in axes:
        scratch += [
            pltpu.VMEM((chunk, part.shape[1]), f32),
            pltpu.VMEM((conds, chunk, part.shape[1]), f32),
            dma((conds,)),
            dma((conds,)),
        ]
    if edges:
        scratch += [dma((4,)), dma((4,))]
    return pl.pallas_call(
        functools.partial(flat_kernel if flat else sum_kernel, axes, bool(edges)),
        out_shape=(shape(part.shape),)
        + tuple(shape((2, HALO, e.shape[1]), e.dtype) for e in edges),
        in_specs=[VMEM] + [ANY] * len(edges),
        out_specs=(VMEM,) * (1 + len(edges)),
        scratch_shapes=scratch,
        compiler_params=pltpu.CompilerParams(
            collective_id=len(axes), has_side_effects=True, vmem_limit_bytes=4 * 1024 * 1024
        ),
        name="sum_" + "_".join(axes),
    )(part, *edges)


def shape(dims, kind=f32):
    return jax.ShapeDtypeStruct(dims, kind)


def shards(mask_pixels, target_bits, perturb, diffusivity, kernels, cond_ids, dose_table):
    rows, length = mask_pixels.shape
    count, band = kernels.shape[1], kernels.shape[-1]
    points = 2 * band
    total = rows + 2 * HALO
    mib = 1024 * 1024
    params = pltpu.CompilerParams(vmem_limit_bytes=12 * mib)
    small, large = angle_parts(length, band, 64)
    left = coarse_tables(band)
    lh, ll = split_np(left)
    wh, wl = split_np(interpolation_table(length, band))
    trans, tab_h, tab_l, local = pl.pallas_call(
        project_kernel,
        out_shape=(
            shape((rows, length)),
            shape((length, points), bf16),
            shape((length, points), bf16),
            shape((points, band)),
        ),
        in_specs=[VMEM] * 4,
        out_specs=(VMEM,) * 4,
        scratch_shapes=[pltpu.VMEM((rows, points), f32)],
        compiler_params=params,
        name="project",
    )(mask_pixels, perturb, small, large)
    mask_band, diff_halo, target_halo = summed(local, ("slab",), (diffusivity, target_bits))
    part = pl.pallas_call(
        image_kernel,
        out_shape=shape((points, band)),
        in_specs=[VMEM] * 2 + [SMEM] * 2 + [ANY] * 2 + [VMEM] * 6,
        out_specs=VMEM,
        scratch_shapes=[
            pltpu.VMEM((points, count * band), bf16),
            pltpu.VMEM((points, count * band), bf16),
            pltpu.VMEM((2 * points, count * band), f32),
            pltpu.VMEM((count, points, 2 * points), f32),
            pltpu.VMEM((points, points), f32),
            pltpu.VMEM((total + 16, length), f32),
            pltpu.VMEM((total + 16, length), f32),
            pltpu.VMEM((total, length), f32),
            pltpu.VMEM((total, length), f32),
            pltpu.VMEM((total, length), f32),
            pltpu.VMEM((total, length), f32),
            pltpu.VMEM((total, length), f32),
            pltpu.VMEM((total, points), bf16),
            pltpu.VMEM((total, points), bf16),
            pltpu.VMEM((rows, points), f32),
            pltpu.VMEM((2 * points, count * band), bf16),
            pltpu.VMEM((2 * points, count * band), bf16),
            pltpu.VMEM((points, 2 * points), bf16),
            pltpu.VMEM((points, 2 * points), bf16),
            pltpu.VMEM((total + 16, length), f32),
            pltpu.VMEM((total, length), jnp.int32),
            pltpu.SemaphoreType.DMA((6,)),
        ],
        compiler_params=pltpu.CompilerParams(vmem_limit_bytes=40 * mib),
        name="image",
    )(
        mask_band, kernels[0], cond_ids, dose_table, diffusivity, target_bits,
        diff_halo, target_halo, lh, ll, wh, wl,
    )
    (grad,) = summed(part, ("cond", "slab"))
    return pl.pallas_call(
        final_kernel,
        out_shape=shape((rows, length)),
        in_specs=[VMEM] * 4,
        out_specs=VMEM,
        scratch_shapes=[
            pltpu.VMEM((rows, points), bf16),
            pltpu.VMEM((rows, points), bf16),
        ],
        compiler_params=params,
        name="final",
    )(grad, trans, tab_h, tab_l)


def solution(mesh):
    placed = (
        P("slab", None),
        P("slab", None),
        P("slab", None),
        P("slab", None),
        P("cond", None, None, None, None),
        P("cond"),
        P(),
    )
    return jax.shard_map(
        shards, mesh=mesh, in_specs=placed, out_specs=P("slab", None), check_vma=False
    )
```

```python
import functools
import math

import jax
import jax.numpy as jnp
import numpy as np
from jax import lax
from jax.experimental import pallas as pl
from jax.experimental.pallas import tpu as pltpu
from jax.sharding import PartitionSpec as P

STEPS = 4
HALO = 2 * STEPS

steepness = 4.0
threshold = 1.0
theta_scale = 2.5

f32 = jnp.float32
bf16 = jnp.bfloat16
VMEM = pl.BlockSpec(memory_space=pltpu.VMEM)
ANY = pl.BlockSpec(memory_space=pl.ANY)
MESH = pl.DeviceIdType.MESH
SMEM = pl.BlockSpec(memory_space=pltpu.SMEM)
NN = (((1,), (0,)), ((), ()))
NT = (((1,), (1,)), ((), ()))
TN = (((0,), (0,)), ((), ()))


def split_np(table):
    high = table.astype(bf16)
    low = (table - high.astype(np.float64)).astype(bf16)
    return jnp.asarray(high), jnp.asarray(low)


def coarse_tables(band):
    points = 2 * band
    turns = np.arange(points)[:, None] * (np.arange(band)[None, :] - band // 2) % points
    angle = turns * (2.0 * math.pi / points)
    cos, sin = np.cos(angle), np.sin(angle)
    return np.concatenate(
        [np.concatenate([cos, -sin], 1), np.concatenate([sin, cos], 1)], 0
    )


def interpolation_table(length, band):
    points = 2 * band
    fine = np.arange(-HALO, length + HALO)
    scale = length // points
    offset = (fine[:, None] - scale * np.arange(points)[None, :]) % length
    freq = np.arange(1, band)
    profile = 1.0 + 2.0 * np.cos(
        (np.arange(length)[:, None] * freq[None, :] % length) * (2.0 * math.pi / length)
    ).sum(1)
    return profile[offset] / points


def angle_parts(length, band, inner):
    freq = np.arange(band) - band // 2
    fine = (np.arange(inner)[:, None] * freq % length) * (2.0 * math.pi / length)
    jump = (np.arange(length // inner)[:, None] * inner * freq % length) * (
        2.0 * math.pi / length
    )
    small = np.stack([np.cos(fine), np.sin(fine)]).astype(np.float32)
    large = np.stack([np.cos(jump), np.sin(jump)]).astype(np.float32)
    return jnp.asarray(small), jnp.asarray(large)


def halves(value):
    high = value.astype(bf16)
    return high, (value - high.astype(f32)).astype(bf16)


def dot3(left, right, dims=NN):
    go = lambda a, b: lax.dot_general(a, b, dims, preferred_element_type=f32)
    return go(left[0], right[0]) + (go(left[0], right[1]) + go(left[1], right[0]))


def project_kernel(mask, perturb, small, large, trans, tab_h, tab_l, band_out, acc):
    rows, length = mask.shape
    band = small.shape[2]
    inner = small.shape[1]
    cos_b, sin_b = small[0], small[1]

    @pl.loop(0, length // inner)
    def _(step):
        cos_a = large[0, pl.ds(step, 1), :]
        sin_a = large[1, pl.ds(step, 1), :]
        at = pl.ds(pl.multiple_of(step * inner, inner), inner)
        for part, value in (
            (0, cos_a * cos_b - sin_a * sin_b),
            (1, -(sin_a * cos_b + cos_a * sin_b)),
        ):
            high, low = halves(value)
            tab_h[at, part * band : (part + 1) * band] = high
            tab_l[at, part * band : (part + 1) * band] = low

    acc[...] = jnp.zeros_like(acc)
    wide = 256

    @pl.loop(0, length // wide)
    def _(step):
        at = pl.ds(pl.multiple_of(step * wide, wide), wide)
        theta = theta_scale * (2.0 * mask[:, at].astype(f32) - 1.0) + perturb[:, at]
        value = jnp.tanh(0.5 * theta)
        trans[:, at] = value
        acc[...] += dot3(halves(value), (tab_h[at, :], tab_l[at, :]))

    mine = pl.ds(pl.multiple_of(lax.axis_index("slab") * rows, rows), rows)
    mixed = dot3((tab_h[mine, :], tab_l[mine, :]), halves(acc[...] / length), TN)
    band_out[0:band, :] = mixed[0:band, 0:band] - mixed[band:, band:]
    band_out[band:, :] = mixed[0:band, band:] + mixed[band:, 0:band]


def bake_sweep(source, dest, coeffs, row_mask):
    east, west, north, south, middle = coeffs
    total, length = middle.shape
    chunks = total // 8
    unroll = max(d for d in range(1, 18) if chunks % d == 0)

    @pl.loop(0, chunks // unroll)
    def _(block):
        for inner in range(unroll):
            index = block * unroll + inner
            at = pl.ds(pl.multiple_of(index * 8, 8), 8)
            put = pl.ds(pl.multiple_of(index * 8 + 8, 8), 8)
            after = pl.ds(pl.multiple_of(index * 8 + 16, 8), 8)
            here = source[put, :]
            above = jnp.where(row_mask == 0, pltpu.roll(source[at, :], 1, 0), pltpu.roll(here, 1, 0))
            below = jnp.where(row_mask == 7, pltpu.roll(source[after, :], 7, 0), pltpu.roll(here, 7, 0))
            dest[put, :] = (
                middle[at, :] * here
                + (north[at, :] * above + south[at, :] * below)
                + (
                    east[at, :] * pltpu.roll(here, length - 1, 1)
                    + west[at, :] * pltpu.roll(here, 1, 1)
                )
            )


def image_kernel(
    band_in, kern, ids, table, diff, target, diff_halo, target_halo, lh, ll, wh, wl, out,
    ah, al, mid, fields, coarse, field, other, east, west, north, south, middle,
    zh, zl, grad, qh, ql, th, tl, cells, goal, sems,
):
    count, _, band, _ = kern.shape
    rows, length = diff.shape
    total = rows + 2 * HALO
    points = 2 * band
    level = table[ids[0]]
    first = pl.multiple_of(lax.axis_index("slab") * rows, rows)
    row_mask = lax.broadcasted_iota(jnp.int32, (8, length), 0)
    chunks = total // 8
    coeffs = (east, west, north, south, middle)

    loads = [
        pltpu.make_async_copy(diff, cells.at[pl.ds(8 + HALO, rows)], sems.at[0]),
        pltpu.make_async_copy(diff_halo.at[0], cells.at[pl.ds(8, HALO)], sems.at[1]),
        pltpu.make_async_copy(diff_halo.at[1], cells.at[pl.ds(8 + HALO + rows, HALO)], sems.at[2]),
        pltpu.make_async_copy(target, goal.at[pl.ds(HALO, rows)], sems.at[3]),
        pltpu.make_async_copy(target_halo.at[0], goal.at[pl.ds(0, HALO)], sems.at[4]),
        pltpu.make_async_copy(target_halo.at[1], goal.at[pl.ds(HALO + rows, HALO)], sems.at[5]),
    ]
    for load in loads:
        load.start()
    blank = jnp.zeros((8, length), f32)
    for ref in (cells, field, other):
        ref[0:8, :] = blank
        ref[total + 8 : total + 16, :] = blank
    th[...] = lh[...].astype(f32).T.astype(bf16)
    tl[...] = ll[...].astype(f32).T.astype(bf16)

    real, imag = band_in[0:band, :], band_in[band:, :]
    for k in range(count):
        cols = slice(k * band, (k + 1) * band)
        kr, ki = kern[k, 0], kern[k, 1]
        ah[0:band, cols], al[0:band, cols] = halves(kr * real - ki * imag)
        ah[band:, cols], al[band:, cols] = halves(kr * imag + ki * real)

    @pl.loop(0, count // 2)
    def _(pair):
        at = pl.ds(pl.multiple_of(pair * points, points), points)
        mid[:, at] = dot3((lh[...], ll[...]), (ah[:, at], al[:, at]))

    coarse[...] = jnp.zeros_like(coarse)

    @pl.loop(0, count)
    def _(k):
        at = pl.ds(pl.multiple_of(k * band, band), band)
        block = jnp.concatenate([mid[0:points, at], mid[points:, at]], axis=1)
        value = dot3(halves(block), (th[...], tl[...])) * (1.0 / band)
        fields[k] = value
        re, im = value[:, :points], value[:, points:]
        coarse[...] += re * re + im * im

    near = pl.ds(first, total)
    zh[...], zl[...] = halves(
        dot3((wh[near, :], wl[near, :]), halves(coarse[...] * (level / count)))
    )
    wide = 256

    @pl.loop(0, length // wide)
    def _(step):
        at = pl.ds(pl.multiple_of(step * wide, wide), wide)
        src = pl.ds(pl.multiple_of(step * wide + HALO, HALO), wide)
        field[8 : 8 + total, at] = dot3((zh[...], zl[...]), (wh[src, :], wl[src, :]), NT)

    for load in loads:
        load.wait()

    @pl.loop(0, chunks)
    def _(index):
        at = pl.ds(pl.multiple_of(index * 8, 8), 8)
        put = pl.ds(pl.multiple_of(index * 8 + 8, 8), 8)
        after = pl.ds(pl.multiple_of(index * 8 + 16, 8), 8)
        here = cells[put, :]
        above = jnp.where(row_mask == 0, pltpu.roll(cells[at, :], 1, 0), pltpu.roll(here, 1, 0))
        below = jnp.where(row_mask == 7, pltpu.roll(cells[after, :], 7, 0), pltpu.roll(here, 7, 0))
        c_e = 0.5 * (here + pltpu.roll(here, length - 1, 1))
        c_w = 0.5 * (here + pltpu.roll(here, 1, 1))
        c_n = 0.5 * (here + above)
        c_s = 0.5 * (here + below)
        east[at, :] = c_e
        west[at, :] = c_w
        north[at, :] = c_n
        south[at, :] = c_s
        middle[at, :] = 1.0 - ((c_e + c_w) + (c_n + c_s))

    @pl.loop(0, 2)
    def _(bake):
        @pl.loop(0, STEPS // 2)
        def _(pair):
            bake_sweep(field, other, coeffs, row_mask)
            bake_sweep(other, field, coeffs, row_mask)

        @pl.when(bake == 0)
        def _():
            @pl.loop(0, chunks)
            def _(index):
                at = pl.ds(pl.multiple_of(index * 8, 8), 8)
                put = pl.ds(pl.multiple_of(index * 8 + 8, 8), 8)
                resist = jax.nn.sigmoid(steepness * (field[put, :] - threshold))
                field[put, :] = (
                    steepness * (resist - goal[at, :].astype(f32)) * resist * (1.0 - resist)
                )

    grad[...] = jnp.zeros_like(grad)

    @pl.loop(0, length // wide)
    def _(step):
        at = pl.ds(pl.multiple_of(step * wide, wide), wide)
        src = pl.ds(pl.multiple_of(step * wide + HALO, HALO), wide)
        grad[...] += dot3(
            halves(field[8 + HALO : 8 + HALO + rows, at]), (wh[src, :], wl[src, :])
        )

    inside = pl.ds(pl.multiple_of(first + HALO, HALO), rows)
    spread = dot3((wh[inside, :], wl[inside, :]), halves(grad[...]), TN)
    coarse[...] = spread * (2.0 * level / count / band)

    @pl.loop(0, count)
    def _(k):
        at = pl.ds(pl.multiple_of(k * band, band), band)
        weight = coarse[...]
        block = fields[k] * jnp.concatenate([weight, weight], axis=1)
        back = dot3(halves(block), (lh[...], ll[...]))
        qh[0:points, at], ql[0:points, at] = halves(back[:, :band])
        qh[points:, at], ql[points:, at] = halves(back[:, band:])

    @pl.loop(0, count // 2)
    def _(pair):
        at = pl.ds(pl.multiple_of(pair * points, points), points)
        mid[0:points, at] = dot3((th[...], tl[...]), (qh[:, at], ql[:, at]))

    sum_re = jnp.zeros((band, band), f32)
    sum_im = jnp.zeros((band, band), f32)
    for k in range(count):
        cols = slice(k * band, (k + 1) * band)
        kr, ki = kern[k, 0], kern[k, 1]
        gr, gi = mid[0:band, cols], mid[band:points, cols]
        sum_re += kr * gr + ki * gi
        sum_im += kr * gi - ki * gr
    out[0:band, :] = sum_re
    out[band:, :] = sum_im


def final_kernel(grad, trans, tab_h, tab_l, out, bh, bl):
    rows, length = trans.shape
    band = grad.shape[1]
    top, low = grad[0:band, :], grad[band:, :]
    matrix = jnp.concatenate(
        [jnp.concatenate([top, low], 1), jnp.concatenate([low, -top], 1)], 0
    )
    mine = pl.ds(pl.multiple_of(lax.axis_index("slab") * rows, rows), rows)
    bh[...], bl[...] = halves(
        dot3((tab_h[mine, :], tab_l[mine, :]), halves(matrix)) * (0.5 / length)
    )
    wide = 256

    @pl.loop(0, length // wide)
    def _(step):
        at = pl.ds(pl.multiple_of(step * wide, wide), wide)
        value = dot3((bh[...], bl[...]), (tab_h[at, :], tab_l[at, :]), NT)
        t = trans[:, at]
        out[:, at] = value * (1.0 - t * t)


def sum_kernel(axes, with_edges, *refs):
    if with_edges:
        part, diff, target, out, diff_halo, target_halo = refs[:6]
        refs = refs[6:]
        edge_send, edge_recv = refs[-2:]
        refs = refs[:-2]
    else:
        part, out = refs[:2]
        refs = refs[2:]
    if "cond" in axes:
        landed, send, recv, mine, crossed, cross_send, cross_recv = refs
    else:
        landed, send, recv = refs
    count = lax.axis_size("slab")
    me = lax.axis_index("slab")
    conds = lax.axis_size("cond")
    chunk = part.shape[0] // count
    peer = [lax.rem(me + d, count) for d in range(count)]
    rank = lax.axis_index("cond")

    barrier = pltpu.get_barrier_semaphore()
    for d in range(1, count):
        pl.semaphore_signal(barrier, inc=1, device_id={"slab": peer[d]}, device_id_type=MESH)
    waits = count - 1
    if "cond" in axes:
        for d in range(1, conds):
            pl.semaphore_signal(
                barrier, inc=1, device_id={"cond": lax.rem(rank + d, conds)}, device_id_type=MESH
            )
        waits += conds - 1
    pl.semaphore_wait(barrier, waits)

    def rows_of(owner):
        return pl.ds(pl.multiple_of(owner * chunk, chunk), chunk)

    first = [
        pltpu.make_async_remote_copy(
            src_ref=part.at[rows_of(peer[d])],
            dst_ref=landed.at[d],
            send_sem=send.at[0, d],
            recv_sem=recv.at[0, d],
            device_id={"slab": peer[d]},
            device_id_type=MESH,
        )
        for d in range(1, count)
    ]
    for copy in first:
        copy.start()
    edges = []
    if with_edges:
        rows = diff.shape[0]
        for number, (source, halo) in enumerate(((diff, diff_halo), (target, target_halo))):
            for side, start, to in ((0, rows - HALO, 1), (1, 0, count - 1)):
                at = 2 * number + side
                edges.append(
                    pltpu.make_async_remote_copy(
                        src_ref=source.at[pl.ds(start, HALO)],
                        dst_ref=halo.at[side],
                        send_sem=edge_send.at[at],
                        recv_sem=edge_recv.at[at],
                        device_id={"slab": peer[to]},
                        device_id_type=MESH,
                    )
                )
        for copy in edges:
            copy.start()
    total = part[rows_of(me), :]
    for d, copy in enumerate(first, 1):
        copy.wait()
        total = total + landed[d]
    if "cond" in axes:
        mine[...] = total
        cross = [
            pltpu.make_async_remote_copy(
                src_ref=mine,
                dst_ref=crossed.at[rank],
                send_sem=cross_send.at[d],
                recv_sem=cross_recv.at[d],
                device_id={"cond": lax.rem(rank + d, conds)},
                device_id_type=MESH,
            )
            for d in range(1, conds)
        ]
        for copy in cross:
            copy.start()
        crossed[rank] = total
        for copy in cross:
            copy.wait()
        total = crossed[0]
        for c in range(1, conds):
            total = total + crossed[c]
    out[rows_of(me), :] = total
    second = [
        pltpu.make_async_remote_copy(
            src_ref=out.at[rows_of(me)],
            dst_ref=out.at[rows_of(me)],
            send_sem=send.at[1, d],
            recv_sem=recv.at[1, d],
            device_id={"slab": peer[d]},
            device_id_type=MESH,
        )
        for d in range(1, count)
    ]
    for copy in second:
        copy.start()
    for copy in second + edges:
        copy.wait()


def flat_kernel(axes, with_edges, *refs):
    if with_edges:
        part, diff, target, out, diff_halo, target_halo, landed, send, recv, edge_send, edge_recv = refs
    else:
        part, out, landed, send, recv = refs
    count = lax.axis_size("slab")
    conds = lax.axis_size("cond")
    me = lax.axis_index("slab")
    rank = lax.axis_index("cond")
    chunk = part.shape[0] // (count * conds)
    peer = [lax.rem(me + d, count) for d in range(count)]
    others = [(c, d) for c in range(conds) for d in range(count) if c or d]

    def place(c, d):
        return {"cond": lax.rem(rank + c, conds), "slab": lax.rem(me + d, count)}

    def rows_of(where):
        owner = where["slab"] * conds + where["cond"]
        return pl.ds(pl.multiple_of(owner * chunk, chunk), chunk)

    barrier = pltpu.get_barrier_semaphore()
    for c, d in others:
        pl.semaphore_signal(barrier, inc=1, device_id=place(c, d), device_id_type=MESH)
    pl.semaphore_wait(barrier, len(others))

    adders = others if "cond" in axes else [(c, d) for c, d in others if c == 0]
    first = []
    for c, d in adders:
        first.append(
            pltpu.make_async_remote_copy(
                src_ref=part.at[rows_of(place(c, d))],
                dst_ref=landed.at[c * count + d],
                send_sem=send.at[0, c * count + d],
                recv_sem=recv.at[0, c * count + d],
                device_id=place(c, d),
                device_id_type=MESH,
            )
        )
    for copy in first:
        copy.start()
    edges = []
    if with_edges:
        rows = diff.shape[0]
        for number, (source, halo) in enumerate(((diff, diff_halo), (target, target_halo))):
            for side, start, to in ((0, rows - HALO, 1), (1, 0, count - 1)):
                at = 2 * number + side
                edges.append(
                    pltpu.make_async_remote_copy(
                        src_ref=source.at[pl.ds(start, HALO)],
                        dst_ref=halo.at[side],
                        send_sem=edge_send.at[at],
                        recv_sem=edge_recv.at[at],
                        device_id={"slab": peer[to]},
                        device_id_type=MESH,
                    )
                )
        for copy in edges:
            copy.start()
    mine = rows_of(place(0, 0))
    total = part[mine, :]
    for (c, d), copy in zip(adders, first):
        copy.wait()
        total = total + landed[c * count + d]
    out[mine, :] = total
    second = [
        pltpu.make_async_remote_copy(
            src_ref=out.at[mine],
            dst_ref=out.at[mine],
            send_sem=send.at[1, c * count + d],
            recv_sem=recv.at[1, c * count + d],
            device_id=place(c, d),
            device_id_type=MESH,
        )
        for c, d in others
    ]
    for copy in second:
        copy.start()
    for copy in second + edges:
        copy.wait()


def summed(part, axes, edges=()):
    count = lax.axis_size("slab")
    conds = lax.axis_size("cond")
    chunk = part.shape[0] // count
    dma = pltpu.SemaphoreType.DMA
    scratch = [pltpu.VMEM((count, chunk, part.shape[1]), f32), dma((2, count)), dma((2, count))]
    flat = "cond" in axes and part.shape[0] % (8 * count * conds) == 0
    if flat:
        owners = count * conds
        scratch = [
            pltpu.VMEM((owners, part.shape[0] // owners, part.shape[1]), f32),
            dma((2, owners)),
            dma((2, owners)),
        ]
    elif "cond" in axes:
        scratch += [
            pltpu.VMEM((chunk, part.shape[1]), f32),
            pltpu.VMEM((conds, chunk, part.shape[1]), f32),
            dma((conds,)),
            dma((conds,)),
        ]
    if edges:
        scratch += [dma((4,)), dma((4,))]
    return pl.pallas_call(
        functools.partial(flat_kernel if flat else sum_kernel, axes, bool(edges)),
        out_shape=(shape(part.shape),)
        + tuple(shape((2, HALO, e.shape[1]), e.dtype) for e in edges),
        in_specs=[VMEM] + [ANY] * len(edges),
        out_specs=(VMEM,) * (1 + len(edges)),
        scratch_shapes=scratch,
        compiler_params=pltpu.CompilerParams(
            collective_id=len(axes), has_side_effects=True, vmem_limit_bytes=4 * 1024 * 1024
        ),
        name="sum_" + "_".join(axes),
    )(part, *edges)


def shape(dims, kind=f32):
    return jax.ShapeDtypeStruct(dims, kind)


def shards(mask_pixels, target_bits, perturb, diffusivity, kernels, cond_ids, dose_table):
    rows, length = mask_pixels.shape
    count, band = kernels.shape[1], kernels.shape[-1]
    points = 2 * band
    total = rows + 2 * HALO
    mib = 1024 * 1024
    params = pltpu.CompilerParams(vmem_limit_bytes=12 * mib)
    small, large = angle_parts(length, band, 64)
    left = coarse_tables(band)
    lh, ll = split_np(left)
    wh, wl = split_np(interpolation_table(length, band))
    trans, tab_h, tab_l, local = pl.pallas_call(
        project_kernel,
        out_shape=(
            shape((rows, length)),
            shape((length, points), bf16),
            shape((length, points), bf16),
            shape((points, band)),
        ),
        in_specs=[VMEM] * 4,
        out_specs=(VMEM,) * 4,
        scratch_shapes=[pltpu.VMEM((rows, points), f32)],
        compiler_params=params,
        name="project",
    )(mask_pixels, perturb, small, large)
    mask_band, diff_halo, target_halo = summed(local, ("slab",), (diffusivity, target_bits))
    part = pl.pallas_call(
        image_kernel,
        out_shape=shape((points, band)),
        in_specs=[VMEM] * 2 + [SMEM] * 2 + [ANY] * 2 + [VMEM] * 6,
        out_specs=VMEM,
        scratch_shapes=[
            pltpu.VMEM((points, count * band), bf16),
            pltpu.VMEM((points, count * band), bf16),
            pltpu.VMEM((2 * points, count * band), f32),
            pltpu.VMEM((count, points, 2 * points), f32),
            pltpu.VMEM((points, points), f32),
            pltpu.VMEM((total + 16, length), f32),
            pltpu.VMEM((total + 16, length), f32),
            pltpu.VMEM((total, length), f32),
            pltpu.VMEM((total, length), f32),
            pltpu.VMEM((total, length), f32),
            pltpu.VMEM((total, length), f32),
            pltpu.VMEM((total, length), f32),
            pltpu.VMEM((total, points), bf16),
            pltpu.VMEM((total, points), bf16),
            pltpu.VMEM((rows, points), f32),
            pltpu.VMEM((2 * points, count * band), bf16),
            pltpu.VMEM((2 * points, count * band), bf16),
            pltpu.VMEM((points, 2 * points), bf16),
            pltpu.VMEM((points, 2 * points), bf16),
            pltpu.VMEM((total + 16, length), f32),
            pltpu.VMEM((total, length), jnp.int32),
            pltpu.SemaphoreType.DMA((6,)),
        ],
        compiler_params=pltpu.CompilerParams(vmem_limit_bytes=40 * mib),
        name="image",
    )(
        mask_band, kernels[0], cond_ids, dose_table, diffusivity, target_bits,
        diff_halo, target_halo, lh, ll, wh, wl,
    )
    (grad,) = summed(part, ("cond", "slab"))
    return pl.pallas_call(
        final_kernel,
        out_shape=shape((rows, length)),
        in_specs=[VMEM] * 4,
        out_specs=VMEM,
        scratch_shapes=[
            pltpu.VMEM((rows, points), bf16),
            pltpu.VMEM((rows, points), bf16),
        ],
        compiler_params=params,
        name="final",
    )(grad, trans, tab_h, tab_l)


def solution(mesh):
    placed = (
        P("slab", None),
        P("slab", None),
        P("slab", None),
        P("slab", None),
        P("cond", None, None, None, None),
        P("cond"),
        P(),
    )
    return jax.shard_map(
        shards, mesh=mesh, in_specs=placed, out_specs=P("slab", None), check_vma=False
    )
```
